32 devices in a mesh: ctx: 16 (over z, y, core), head: 2 (over x).
Axes of the slice: x: 2, y: 2, z: 4, core: 2. Of those that a mesh axis runs over, the one named last changes fastest.
Arguments:
- queries: bfloat16 [8192, 8, 4, 128], P('ctx', None, 'head'), may hold values from -6 to 6
- key_heads: bfloat16 [8192, 8, 128], P('ctx'), may hold values from -6 to 6
- value_heads: bfloat16 [8192, 8, 128], P('ctx'), may hold values from -6 to 6
- out_grad: bfloat16 [8192, 8, 4, 128], P('ctx', None, 'head'), may hold values from -6 to 6
- doc_ids: int32 [8192], P('ctx'), may hold values from 0 to 31, never falling along the last dimension, each value on 1 to 2048 neighbouring positions
Outputs:
- query_grad: bfloat16 [8192, 8, 4, 128], P('ctx', None, 'head')
- key_grad: bfloat16 [8192, 8, 128], P('ctx', 'head')
- value_grad: bfloat16 [8192, 8, 128], P('ctx', 'head')
The draws below stay inside these ranges and needn't reach their ends.
Inputs may be any that keep to these rules, and one draw needn't show every extreme that they name: `doc_ids`: ids never fall along the sequence; a document has at most 2048 tokens.
All inputs are finite; a program needn't handle non-finite values.
Results may differ from the reference program's by a relative error of at most 0.012.
Values may be sent and summed in bfloat16 or wider, within the bound.
No kernel may reach another device: no remote copies, remote signals or barrier semaphores. Data moves between devices by JAX's collectives and lax.ppermute only.
A program may use at most 64 MiB of HBM per device.

```python
import math
import jax
import jax.numpy as jnp
import numpy as np
from jax import lax

KV = 8
GROUP = 4
HD = 128
WINDOW = 256
TOK_DEV = 512
TOKENS = 8192
DOCS = 32
N_CTX = 16


def draw_queries(key, part):
    own_key = jax.random.fold_in(key, 1)
    result = jnp.clip(jax.random.normal(own_key, (TOKENS, KV, GROUP, HD), jnp.float32), -6.0, 6.0)
    return result.astype(jnp.bfloat16)


def draw_key_heads(key, part):
    own_key = jax.random.fold_in(key, 2)
    result = jnp.clip(jax.random.normal(own_key, (TOKENS, KV, HD), jnp.float32), -6.0, 6.0)
    return result.astype(jnp.bfloat16)


def block_levels(key, extent, shards, smallest, largest):
    factor_of = 1.0
    for position, blocks in shards:
        draws = jax.random.uniform(jax.random.fold_in(jax.random.fold_in(key, 6), position), (blocks,), jnp.float32, smallest / len(shards), largest / len(shards))
        factor_of = factor_of * jnp.repeat(jnp.exp(draws), extent[position] // blocks).reshape((-1,) + (1,) * (len(extent) - 1 - position))
    return factor_of


def profile(count, total, limit, lean):
    weights = [(1 << 20) // math.isqrt(rank ** lean) + 1 for rank in range(2, count + 1)]
    spare, holding = total - limit - (count - 1), [1] * (count - 1)
    while spare > 0:
        free = [i for i in range(count - 1) if holding[i] < limit]
        whole, remaining = sum([weights[i] for i in free]), spare
        for i in free:
            extra = min(limit - holding[i], max(1, remaining * weights[i] // whole), spare)
            holding[i] = holding[i] + extra
            spare = spare - extra
    return np.array([limit] + holding)


def ragged_sizes(key, count, total, reach, lean):
    if count == 2:
        one = jax.random.randint(key, (), max(1, total - reach), min(reach, total - 1) + 1)
        return jnp.stack([one, total - one])
    lengths = jnp.asarray(profile(count, total, reach, lean), jnp.int32)
    twos = (count - 1) // 2
    giver, sink = lengths[1:1 + 2 * twos:2], lengths[2:2 + 2 * twos:2]
    margin = jnp.minimum(giver - 1, reach - sink)
    moved = jax.random.randint(jax.random.fold_in(key, 1), (twos,), 0, 1 << 20) % (margin + 1)
    lengths = lengths.at[1:1 + 2 * twos:2].set(giver - moved).at[2:2 + 2 * twos:2].set(sink + moved)
    return lengths[jax.random.permutation(jax.random.fold_in(key, 2), count)]


def bell_draw(stream_key, shape, scale, limit, pieces=(), kind=jnp.bfloat16):
    array = scale * jax.random.normal(stream_key, shape, jnp.float32)
    if pieces:
        array = array * block_levels(stream_key, shape, pieces, -0.22, 0.18)
    return jnp.clip(array, -limit, limit).astype(kind)


def setup_inputs(seed: int = 0) -> dict:
    key_list = jax.random.split(jax.random.key(seed), 6)
    queries = draw_queries(jax.random.fold_in(key_list[5], 71), 0)
    key_heads = draw_key_heads(jax.random.fold_in(key_list[5], 71), 0)
    value_heads = bell_draw(key_list[2], (TOKENS, KV, HD), 1.0, 6.0, ((0, 16),))
    out_grad = bell_draw(key_list[3], (TOKENS, KV, GROUP, HD), 1.0, 6.0, ((0, 16), (2, 2)))
    doc_ids = jnp.searchsorted(jnp.cumsum(ragged_sizes(key_list[4], DOCS, TOKENS, 4 * TOK_DEV, 2)), jnp.arange(TOKENS), side="right").astype(jnp.int32)
    return dict(queries=queries, key_heads=key_heads, value_heads=value_heads, out_grad=out_grad, doc_ids=doc_ids)


def window_grads(query_blk, key_win, value_win, grad_blk, pos_query, pos_key, doc_query, doc_key):
    scaling = 1.0 / (HD ** 0.5)
    lag_rows = pos_query[:, None] - pos_key[None, :]
    visible = (lag_rows >= 0) & (lag_rows < WINDOW) & (doc_query[:, None] == doc_key[None, :]) & (pos_key[None, :] >= 0)
    query_f = query_blk.astype(jnp.float32)
    key_f = key_win.astype(jnp.float32)
    value_f = value_win.astype(jnp.float32)
    grad_f = grad_blk.astype(jnp.float32)
    scores = jnp.einsum("lngd,mnd->nglm", query_f, key_f) * scaling
    scores = jnp.where(visible[None, None], scores, -jnp.inf)
    top_score = jnp.max(scores, axis=-1, keepdims=True)
    weights = jnp.exp(scores - top_score)
    attn_prob = weights / jnp.sum(weights, axis=-1, keepdims=True)
    prob_low = lax.optimization_barrier(attn_prob.astype(jnp.bfloat16)).astype(jnp.float32)
    attended = jnp.einsum("nglm,mnd->lngd", prob_low, value_f)
    row_delta = jnp.sum(grad_f * attended, axis=-1)
    grad_prob = jnp.einsum("lngd,mnd->nglm", grad_f, value_f)
    grad_scores = attn_prob * (grad_prob - jnp.transpose(row_delta, (1, 2, 0))[..., None])
    grad_low = lax.optimization_barrier(grad_scores.astype(jnp.bfloat16)).astype(jnp.float32)
    query_part = (jnp.einsum("nglm,mnd->lngd", grad_low, key_f) * scaling).astype(jnp.bfloat16)
    key_part = jnp.einsum("nglm,lngd->mnd", grad_low, query_f) * scaling
    value_part = jnp.einsum("nglm,lngd->mnd", prob_low, grad_f)
    return query_part, key_part, value_part


def reference(queries, key_heads, value_heads, out_grad, doc_ids):
    window_rows = TOK_DEV + WINDOW
    pad_keys = jnp.concatenate([jnp.zeros((WINDOW, KV, HD), key_heads.dtype), key_heads], 0)
    pad_values = jnp.concatenate([jnp.zeros((WINDOW, KV, HD), value_heads.dtype), value_heads], 0)
    doc_all = doc_ids.astype(jnp.int32)
    pad_docs = jnp.concatenate([jnp.full((WINDOW,), -1, jnp.int32), doc_all], 0)
    offsets = jnp.arange(window_rows, dtype=jnp.int32)
    query_rows = jnp.arange(TOK_DEV, dtype=jnp.int32)

    def scan_step(loop_state, block_idx):
        key_acc, value_acc = loop_state
        anchor = (block_idx * TOK_DEV).astype(jnp.int32)
        query_blk = lax.dynamic_slice_in_dim(queries, anchor, TOK_DEV, 0)
        grad_blk = lax.dynamic_slice_in_dim(out_grad, anchor, TOK_DEV, 0)
        key_win = lax.dynamic_slice_in_dim(pad_keys, anchor, window_rows, 0)
        value_win = lax.dynamic_slice_in_dim(pad_values, anchor, window_rows, 0)
        doc_query = lax.dynamic_slice_in_dim(doc_all, anchor, TOK_DEV, 0)
        doc_key = lax.dynamic_slice_in_dim(pad_docs, anchor, window_rows, 0)
        pos_query = anchor + query_rows
        pos_key = anchor - WINDOW + offsets
        query_part, key_part, value_part = window_grads(query_blk, key_win, value_win, grad_blk, pos_query, pos_key, doc_query, doc_key)
        key_acc = lax.dynamic_update_slice_in_dim(key_acc, lax.dynamic_slice_in_dim(key_acc, anchor, window_rows, 0) + key_part, anchor, 0)
        value_acc = lax.dynamic_update_slice_in_dim(value_acc, lax.dynamic_slice_in_dim(value_acc, anchor, window_rows, 0) + value_part, anchor, 0)
        return (key_acc, value_acc), query_part

    initial = (jnp.zeros((TOKENS + WINDOW, KV, HD), jnp.float32), jnp.zeros((TOKENS + WINDOW, KV, HD), jnp.float32))
    (key_acc, value_acc), query_parts = lax.scan(scan_step, initial, jnp.arange(N_CTX, dtype=jnp.int32))
    query_grad = query_parts.reshape(TOKENS, KV, GROUP, HD)
    return query_grad, key_acc[WINDOW:].astype(jnp.bfloat16), value_acc[WINDOW:].astype(jnp.bfloat16)
```

```python
import functools

import jax
import jax.numpy as jnp
from jax import lax
from jax.experimental import pallas as pl
from jax.experimental.pallas import tpu as pltpu
from jax.sharding import PartitionSpec as P

WINDOW = 256
CHUNK = 128
LOG2E = 1.4426950408889634
F32 = jnp.float32
BF16 = jnp.bfloat16


def dot(a, b, contract):
    return lax.dot_general(a, b, ((contract[0], contract[1]), ((), ())), preferred_element_type=F32)


def chunk_grads(q, do, k, v, kt, low):
    cols = q.shape[0]
    group = cols // CHUNK
    scale = 1.0 / q.shape[1] ** 0.5
    rows = lax.broadcasted_iota(jnp.int32, (k.shape[0], cols), 0)
    last = lax.div(lax.broadcasted_iota(jnp.int32, (1, cols), 1), jnp.int32(group)) + WINDOW
    scores = dot(k, q, ((1,), (1,)))
    grad_prob = dot(v, do, ((1,), (1,)))
    scores = jnp.where((rows >= low) & (rows <= last), scores, -1e30)
    top = jnp.max(scores, axis=0, keepdims=True)
    weights = jnp.exp2((scores - top) * (scale * LOG2E))
    total = jnp.sum(weights, axis=0, keepdims=True)
    prob = weights * (1.0 / total)
    delta = jnp.sum(prob * grad_prob, axis=0, keepdims=True)
    prob_low = prob.astype(BF16)
    grad_low = (prob * (grad_prob - delta)).astype(BF16)
    query_grad = dot(kt, grad_low, ((1,), (0,))) * scale
    return (
        query_grad.T.astype(BF16),
        dot(grad_low, q, ((1,), (0,))),
        dot(prob_low, do, ((1,), (0,))),
    )


def kernel(head_ref, *refs, chunks, first, halo, carry, emit, aliased):
    it = iter(refs)
    low_ref, q_ref, do_ref, kv_ref = next(it), next(it), next(it), next(it)
    halo_ref = next(it) if halo else None
    carry_ref = next(it) if carry else None
    if aliased:
        next(it)
    dq_ref = next(it)
    own_ref = next(it)
    back_ref = next(it) if halo else None
    acc = next(it)
    win = next(it) if halo else None
    head_size = q_ref.shape[-1]
    group = q_ref.shape[-2]
    cols = CHUNK * group
    scale = 1.0 / head_size**0.5
    span = kv_ref.shape[1]
    if halo:
        win[:, :WINDOW] = halo_ref[...]
        win[:, WINDOW:] = kv_ref[...]
        src = win
    else:
        src = kv_ref
    acc[...] = jnp.zeros_like(acc)
    kt = src[0].T
    for slot, chunk in enumerate(chunks):
        start = chunk * CHUNK - WINDOW - first
        keys = slice(start, start + WINDOW + CHUNK)
        own = slice(slot * CHUNK, (slot + 1) * CHUNK)
        q = q_ref[own].reshape(cols, head_size)
        do = do_ref[own].reshape(cols, head_size)
        low = low_ref[slot : slot + 1, :]
        dq, dk, dv = chunk_grads(q, do, src[0, keys], src[1, keys], kt[:, keys], low)
        dq_ref[own] = dq.reshape(CHUNK, group, head_size)
        acc[0, keys] += dk
        acc[1, keys] += dv
    off = 0
    if halo:
        back_ref[0] = (acc[0, :WINDOW] * scale).astype(BF16)
        back_ref[1] = acc[1, :WINDOW].astype(BF16)
        off = WINDOW
    for i, factor in ((0, scale), (1, 1.0)):
        value = acc[i, off:] * factor
        if carry:
            value = value + carry_ref[i]
        own_ref[i] = value.astype(own_ref.dtype)


def attend(head, low, queries, out_grad, kv, halo, carry, query_grad, chunks, heads, emit):
    tokens, kv_count, group, head_size = queries.shape
    rows = len(chunks) * CHUNK
    row_block = chunks[0] * CHUNK // rows
    has_halo = halo is not None
    first = -WINDOW if has_halo else 0
    top = (chunks[-1] + 1) * CHUNK
    span = top
    q_spec = pl.BlockSpec((rows, None, group, head_size), lambda n, h: (row_block, n + h[0], 0, 0))
    part = lambda r, block=0: pl.BlockSpec((2, None, r, head_size), lambda n, h: (0, n, block, 0))
    in_specs = [
        pl.BlockSpec(low.shape, lambda n, h: (0, 0)),
        q_spec,
        q_spec,
        pl.BlockSpec((2, None, span, head_size), lambda n, h: (0, n + h[0], 0, 0)),
    ]
    operands = [low, queries, out_grad, kv]
    if has_halo:
        in_specs.append(part(WINDOW))
        operands.append(halo)
    if carry is not None:
        in_specs.append(part(span))
        operands.append(carry)
    aliases = {}
    if query_grad is not None:
        aliases = {1 + len(operands): 0}
        in_specs.append(pl.BlockSpec(memory_space=pl.ANY))
        operands.append(query_grad)
    out_specs = [q_spec, part(span)]
    out_shape = [
        jax.ShapeDtypeStruct(queries.shape, BF16),
        jax.ShapeDtypeStruct((2, heads, span, head_size), emit),
    ]
    window = span + (WINDOW if has_halo else 0)
    scratch = [pltpu.VMEM((2, window, head_size), F32)]
    if has_halo:
        out_specs.append(part(WINDOW))
        out_shape.append(jax.ShapeDtypeStruct((2, heads, WINDOW, head_size), BF16))
        scratch.append(pltpu.VMEM((2, window, head_size), BF16))
    flops = heads * len(chunks) * 5 * 2 * CHUNK * group * (WINDOW + CHUNK) * head_size
    return pl.pallas_call(
        functools.partial(
            kernel,
            chunks=chunks,
            first=first,
            halo=has_halo,
            carry=carry is not None,
            emit=emit,
            aliased=query_grad is not None,
        ),
        grid_spec=pltpu.PrefetchScalarGridSpec(
            num_scalar_prefetch=1,
            grid=(heads,),
            in_specs=in_specs,
            out_specs=out_specs,
            scratch_shapes=scratch,
        ),
        out_shape=out_shape,
        input_output_aliases=aliases,
        compiler_params=pltpu.CompilerParams(vmem_limit_bytes=32 * 1024 * 1024),
        cost_estimate=pl.CostEstimate(
            flops=flops, bytes_accessed=heads * rows * group * head_size * 8, transcendentals=0
        ),
    )(head, *operands)


def shift(block, axis, distance):
    devices = range(lax.axis_size(axis))
    return lax.ppermute(block, axis, [(i - distance, i) for i in devices if i - distance in devices])


def swap(block):
    return lax.ppermute(block, "head", [(0, 1), (1, 0)])


def on_device(queries, key_heads, value_heads, out_grad, doc_ids):
    tokens, kv_count, group, _ = queries.shape
    half = kv_count // 2
    mine = lax.axis_index("head") * half
    other = half - mine
    chunk_count = tokens // CHUNK
    split = WINDOW // CHUNK
    kv = jnp.stack([key_heads.transpose(1, 0, 2), value_heads.transpose(1, 0, 2)])
    tail = kv[:, :, tokens - WINDOW :]
    halo_other = shift(lax.dynamic_slice_in_dim(tail, other, half, 1), "ctx", 1)
    prev_docs = shift(doc_ids[tokens - WINDOW :], "ctx", 1)
    halo_mine = shift(lax.dynamic_slice_in_dim(tail, mine, half, 1), "ctx", 1)

    token = jnp.arange(tokens, dtype=jnp.int32)
    lower = jnp.sum((doc_ids[None, :] < doc_ids[:, None]).astype(jnp.int32), axis=1)
    prev_docs = jnp.where(lax.axis_index("ctx") == 0, -1, prev_docs)
    before = jnp.sum((prev_docs[None, :] < doc_ids[:WINDOW, None]).astype(jnp.int32), axis=1)

    def columns(low):
        low = jnp.repeat(low, group).reshape(-1, CHUNK * group)
        base = jnp.arange(low.shape[0], dtype=jnp.int32)[:, None] * CHUNK
        return low - base

    low_late = columns(jnp.maximum(token + 1, lower + WINDOW)[WINDOW:] - WINDOW)
    low_early = columns(jnp.maximum(token[:WINDOW] + 1, lower[:WINDOW] + before))

    head_other = jnp.reshape(other, (1,))
    head_mine = jnp.reshape(mine, (1,))
    late = tuple(range(split, chunk_count))
    early = tuple(range(split))
    query_grad, part_other = attend(
        head_other, low_late, queries, out_grad, kv, None, None, None, late, half, F32
    )
    query_grad, first_other, back_other = attend(
        head_other, low_early, queries, out_grad, kv, halo_other, part_other, query_grad, early, half, BF16
    )
    back_other = shift(back_other, "ctx", -1)
    first_other = swap(first_other)
    query_grad, part_mine, back_mine = attend(
        head_mine,
        jnp.concatenate([low_early, low_late - 0]),
        queries,
        out_grad,
        kv,
        halo_mine,
        None,
        query_grad,
        early + late,
        half,
        F32,
    )
    last_other = part_other[:, :, WINDOW:]
    last_other = last_other.at[:, :, tokens - 2 * WINDOW :].add(back_other.astype(F32))
    last_other = swap(last_other.astype(BF16))
    back_mine = shift(back_mine, "ctx", -1)
    total = part_mine + jnp.concatenate([first_other, last_other], 2).astype(F32)
    total = total.at[:, :, tokens - WINDOW :].add(back_mine.astype(F32))
    total = total.astype(BF16).transpose(0, 2, 1, 3)
    return query_grad, total[0], total[1]


def solution(mesh):
    in_specs = (
        P("ctx", None, "head", None),
        P("ctx", None, None),
        P("ctx", None, None),
        P("ctx", None, "head", None),
        P("ctx"),
    )
    out_specs = (P("ctx", None, "head", None), P("ctx", "head", None), P("ctx", "head", None))
    return jax.shard_map(on_device, mesh=mesh, in_specs=in_specs, out_specs=out_specs, check_vma=False)
```

```python
import functools

import jax
import jax.numpy as jnp
from jax import lax
from jax.experimental import pallas as pl
from jax.experimental.pallas import tpu as pltpu
from jax.sharding import PartitionSpec as P

WINDOW = 256
CHUNK = WINDOW // 2
PAD = 8
LOG2E = 1.4426950408889634
F32 = jnp.float32
BF16 = jnp.bfloat16
VMEM = pl.BlockSpec(memory_space=pltpu.VMEM)
SMEM = pl.BlockSpec(memory_space=pltpu.SMEM)
ANY = pl.BlockSpec(memory_space=pl.ANY)
MIB = 1024 * 1024


def dot(a, b, contract):
    return lax.dot_general(a, b, (((contract[0],), (contract[1],)), ((), ())), preferred_element_type=F32)


def params(limit):
    return pltpu.CompilerParams(vmem_limit_bytes=limit * MIB)


def count_smaller(column, row):
    return jnp.sum((column < row).astype(F32), axis=0, keepdims=True)


def prepare_kernel(sel_ref, key_ref, value_ref, docs_ref, kv_ref, other_ref, mine_ref):
    half = other_ref.shape[1]
    tokens = key_ref.shape[0]
    kv_ref[0] = jnp.transpose(key_ref[...], (1, 0, 2))
    kv_ref[1] = jnp.transpose(value_ref[...], (1, 0, 2))
    tail = docs_ref[...].astype(BF16)
    for part, out in ((0, other_ref), (1, mine_ref)):
        first = sel_ref[part] * half
        for i in range(2):
            for h in range(half):
                out[i, h, :WINDOW] = kv_ref[i, first + h, tokens - WINDOW :]
                out[i, h, WINDOW:] = tail


def half_grads(chunks, get_q, get_do, get_keys, get_low, scale, group, put_dq, put_block):
    cols = CHUNK * group
    row = lax.broadcasted_iota(jnp.int32, (CHUNK, cols), 0)
    token = lax.broadcasted_iota(jnp.int32, (CHUNK, cols), 1) & (CHUNK - 1)
    old = row > token
    old_low = old.astype(F32).astype(BF16)
    new_low = 1 - old_low
    position = jnp.where(old, row, row + 2 * CHUNK)
    middle = row + CHUNK
    qs, dos, dqs = {}, {}, {}
    heads = None
    sums = {}
    state = {}

    def fetch(c):
        qs[c], dos[c] = get_q(c), get_do(c)

    fetch(0)
    heads = qs[0].shape[0] // group
    items = [(c, h) for c in range(len(chunks)) for h in range(heads)]

    def scores(item):
        c, h = item
        if c not in qs:
            fetch(c)
        q = qs[c][h * group : (h + 1) * group].reshape(cols, -1)
        do = dos[c][h * group : (h + 1) * group].reshape(cols, -1)
        k, v = get_keys(h, c)
        state[item] = (q, do, k, dot(k, q, (1, 1)), dot(v, do, (1, 1)))

    def soft(item):
        c, h = item
        q, do, k, s, dp = state[item]
        low = get_low(c)
        s = [
            jnp.where(position >= low, jnp.where(old, s[:CHUNK], s[2 * CHUNK :]), -1e30),
            jnp.where(middle >= low, s[CHUNK : 2 * CHUNK], -1e30),
        ]
        dp = [jnp.where(old, dp[:CHUNK], dp[2 * CHUNK :]), dp[CHUNK : 2 * CHUNK]]
        top = functools.reduce(jnp.maximum, [jnp.max(x, axis=0, keepdims=True) for x in s])
        w = [jnp.exp2((x - top) * (scale * LOG2E)) for x in s]
        total = sum(jnp.sum(x, axis=0, keepdims=True) for x in w)
        inverse = 1.0 / total
        p = [x * inverse for x in w]
        delta = sum(jnp.sum(x * y, axis=0, keepdims=True) for x, y in zip(p, dp))
        ds = [(x * (y - delta)).astype(BF16) for x, y in zip(p, dp)]
        p = [x.astype(BF16) for x in p]
        p = jnp.concatenate([p[0] * old_low, p[1], p[0] * new_low], 0)
        ds = jnp.concatenate([ds[0] * old_low, ds[1], ds[0] * new_low], 0)
        state[item] = (q, do, k, p, ds)

    def grads(item):
        c, h = item
        q, do, k, p, ds = state.pop(item)
        dv = dot(p, do, (1, 0))
        dk = dot(ds, q, (1, 0))
        for b in range(3):
            rows = slice(b * CHUNK, (b + 1) * CHUNK)
            key = (h, c + b)
            new = (dk[rows], dv[rows])
            if key in sums:
                new = (sums[key][0] + new[0], sums[key][1] + new[1])
            sums[key] = new
            if b == 0 or c == len(chunks) - 1:
                put_block(h, c + b, *sums.pop(key))
        dqs[item] = (dot(k.T, ds, (1, 0)) * scale).T.astype(BF16).reshape(group, CHUNK, -1)
        if h == heads - 1:
            full = jnp.concatenate([dqs.pop((c, i)) for i in range(heads)], 0)
            put_dq(c, jnp.transpose(full, (1, 0, 2)))

    scores(items[0])
    for n, item in enumerate(items):
        if n + 1 < len(items):
            scores(items[n + 1])
        if n:
            grads(items[n - 1])
        soft(item)
    grads(items[-1])


def store_rows(buf, sem, slot, dq_ref, rows, where):
    return pltpu.make_async_copy(buf.at[slot], dq_ref.at[rows, where, :], sem.at[slot])


def late_kernel(sel_ref, low_ref, q_ref, do_ref, kv_ref, dq_ref, part_ref, buf, sem, *, chunks, group):
    half = part_ref.shape[2]
    rows = half * group
    scale = 1.0 / q_ref.shape[-1] ** 0.5

    def one(n, carry):
        sel = sel_ref[n]
        where = pl.ds(pl.multiple_of(sel * rows, rows), rows)

        def tokens(c):
            return slice(chunks[c] * CHUNK, (chunks[c] + 1) * CHUNK)

        def put_dq(c, value):
            slot = n * len(chunks) + c
            buf[slot] = value
            store_rows(buf, sem, slot, dq_ref, tokens(c), where).start()

        def get_keys(h, c):
            keys = slice((chunks[c] - 2) * CHUNK, (chunks[c] + 1) * CHUNK)
            return kv_ref[0, sel * half + h, keys], kv_ref[1, sel * half + h, keys]

        def put_block(h, b, dk, dv):
            block = slice((chunks[0] - 2 + b) * CHUNK, (chunks[0] - 1 + b) * CHUNK)
            part_ref[n, 0, h, block] = dk * scale
            part_ref[n, 1, h, block] = dv

        half_grads(
            chunks,
            lambda c: jnp.transpose(q_ref[tokens(c), where, :], (1, 0, 2)),
            lambda c: jnp.transpose(do_ref[tokens(c), where, :], (1, 0, 2)),
            get_keys,
            lambda c: low_ref[chunks[c] : chunks[c] + 1, :],
            scale,
            group,
            put_dq,
            put_block,
        )
        return carry

    lax.fori_loop(0, 2, one, 0)
    for n in range(2):
        for c, chunk in enumerate(chunks):
            rows_of = slice(chunk * CHUNK, (chunk + 1) * CHUNK)
            store_rows(buf, sem, n * len(chunks) + c, dq_ref, rows_of, slice(0, rows)).wait()


def early_kernel(
    sel_ref, docs_ref, low_ref, q_ref, do_ref, kv_ref, halo_ref, part_ref, dq_in, dq_ref, own_ref, back_ref, buf, sem, *, group, n
):
    half = own_ref.shape[1]
    rows = half * group
    scale = 1.0 / q_ref.shape[-1] ** 0.5
    sel = sel_ref[n]
    where = pl.ds(pl.multiple_of(sel * rows, rows), rows)
    before = jnp.where(sel_ref[2] == 0, -1.0, halo_ref[0, 0, WINDOW:].astype(F32)).T
    lows = []
    for c in range(2):
        docs = docs_ref[c : c + 1, :]
        count = count_smaller(before[:, :1], docs) + count_smaller(before[:, 1:2], docs)
        count = jnp.concatenate([count] * group, 1)
        lows.append(low_ref[c : c + 1, :] - WINDOW + count.astype(jnp.int32))

    def tokens(c):
        return slice(c * CHUNK, (c + 1) * CHUNK)

    def put_dq(c, value):
        buf[c] = value
        store_rows(buf, sem, c, dq_ref, tokens(c), where).start()

    def get_keys(h, c):
        return tuple(
            jnp.concatenate(
                [halo_ref[i, h, c * CHUNK : WINDOW], kv_ref[i, sel * half + h, : (c + 1) * CHUNK]], 0
            )
            for i in range(2)
        )

    def put_block(h, b, dk, dv):
        dk = dk * scale
        if b < 2:
            block = slice(b * CHUNK, (b + 1) * CHUNK)
            back_ref[0, h, block] = dk.astype(BF16)
            back_ref[1, h, block] = dv.astype(BF16)
        else:
            block = slice((b - 2) * CHUNK, (b - 1) * CHUNK)
            own_ref[0, h, block] = (dk + part_ref[n, 0, h, block]).astype(own_ref.dtype)
            own_ref[1, h, block] = (dv + part_ref[n, 1, h, block]).astype(own_ref.dtype)

    half_grads(
        (0, 1),
        lambda c: jnp.transpose(q_ref[tokens(c), where, :], (1, 0, 2)),
        lambda c: jnp.transpose(do_ref[tokens(c), where, :], (1, 0, 2)),
        get_keys,
        lambda c: lows[c],
        scale,
        group,
        put_dq,
        put_block,
    )
    for c in range(2):
        store_rows(buf, sem, c, dq_ref, tokens(c), where).wait()


def finish_kernel(first_ref, first_in, part_ref, last_in, back_in, dk_ref, dv_ref, *, n):
    tokens = dk_ref.shape[0]
    for i, out in ((0, dk_ref), (1, dv_ref)):
        value = first_ref[i] + first_in[i].astype(F32)
        out[:WINDOW] = jnp.transpose(value.astype(BF16), (1, 0, 2))
        late = part_ref[n, i, :, WINDOW:] + last_in[i].astype(F32)
        value = late[:, tokens - 2 * WINDOW :] + back_in[i].astype(F32)
        if tokens > 2 * WINDOW:
            value = jnp.concatenate([late[:, : tokens - 2 * WINDOW], value], 1)
        out[WINDOW:] = jnp.transpose(value.astype(BF16), (1, 0, 2))


def shift(block, axis, distance):
    devices = range(lax.axis_size(axis))
    return lax.ppermute(block, axis, [(i - distance, i) for i in devices if i - distance in devices])


def swap(block):
    return lax.ppermute(block, "head", [(0, 1), (1, 0)])


def on_device(queries, key_heads, value_heads, out_grad, doc_ids):
    tokens, kv_count, group, size = queries.shape
    half = kv_count // 2
    chunks = tokens // CHUNK
    shape = jax.ShapeDtypeStruct
    head = lax.axis_index("head")
    sel = jnp.stack([1 - head, head, lax.axis_index("ctx")]).astype(jnp.int32)
    rows = queries.reshape(tokens, kv_count * group, size)
    grads = out_grad.reshape(tokens, kv_count * group, size)
    docs = doc_ids.reshape(chunks, CHUNK).astype(F32)
    tail = jnp.pad(docs[chunks - 2 :], ((0, PAD - 2), (0, 0)))
    halo_shape = shape((2, half, WINDOW + PAD, size), BF16)
    kv, halo_other, halo_mine = pl.pallas_call(
        prepare_kernel,
        in_specs=[SMEM, VMEM, VMEM, VMEM],
        out_specs=[VMEM] * 3,
        out_shape=[shape((2, kv_count, tokens, size), BF16), halo_shape, halo_shape],
        compiler_params=params(16),
        name="prepare",
    )(sel, key_heads, value_heads, tail)
    halo_other = shift(halo_other, "ctx", 1)
    halo_mine = shift(halo_mine, "ctx", 1)

    smaller = jnp.sum((doc_ids[:, None] < doc_ids[None, :]).astype(jnp.int32), axis=0)
    low = smaller.reshape(chunks, CHUNK) + (WINDOW - CHUNK * jnp.arange(chunks, dtype=jnp.int32)[:, None])
    low = jnp.concatenate([low] * group, 1)

    def cost(n):
        work = n * 10 * CHUNK * group * (WINDOW + CHUNK) * size
        return pl.CostEstimate(flops=work * 10, bytes_accessed=n * CHUNK * group * size * 8, transcendentals=0)

    def staging(n):
        return [pltpu.VMEM((n, CHUNK, half * group, size), BF16), pltpu.SemaphoreType.DMA((n,))]

    late = tuple(range(2, chunks))
    query_grad, part = pl.pallas_call(
        functools.partial(late_kernel, chunks=late, group=group),
        in_specs=[SMEM] + [VMEM] * 4,
        out_specs=[ANY, VMEM],
        out_shape=[shape(rows.shape, BF16), shape((2, 2, half, tokens, size), F32)],
        scratch_shapes=staging(2 * len(late)),
        compiler_params=params(24),
        cost_estimate=cost(kv_count * len(late)),
        name="late",
    )(sel, low, rows, grads, kv)

    def early(n, halo, query_grad, emit):
        return pl.pallas_call(
            functools.partial(early_kernel, group=group, n=n),
            in_specs=[SMEM] + [VMEM] * 7 + [ANY],
            out_specs=[ANY, VMEM, VMEM],
            scratch_shapes=staging(2),
            out_shape=[
                shape(rows.shape, BF16),
                shape((2, half, WINDOW, size), emit),
                shape((2, half, WINDOW, size), BF16),
            ],
            input_output_aliases={8: 0},
            compiler_params=params(24),
            cost_estimate=cost(half * 2),
            name="early",
        )(sel, docs, low, rows, grads, kv, halo, part, query_grad)

    query_grad, first_other, back_other = early(0, halo_other, query_grad, BF16)
    first_other = swap(first_other)
    back_other = shift(back_other, "ctx", -1)
    query_grad, first_mine, back_mine = early(1, halo_mine, query_grad, F32)
    back_mine = shift(back_mine, "ctx", -1)
    back_other, _ = lax.optimization_barrier((back_other, first_mine))
    last_other = part[0, :, :, WINDOW:]
    last_other = last_other.at[:, :, tokens - 2 * WINDOW :].add(back_other.astype(F32))
    last_other = swap(last_other.astype(BF16))
    out = shape((tokens, half, size), BF16)
    key_grad, value_grad = pl.pallas_call(
        functools.partial(finish_kernel, n=1),
        in_specs=[VMEM] * 5,
        out_specs=[VMEM] * 2,
        out_shape=[out, out],
        compiler_params=params(16),
        name="finish",
    )(first_mine, first_other, part, last_other, back_mine)
    return query_grad.reshape(queries.shape), key_grad, value_grad


def solution(mesh):
    in_specs = (
        P("ctx", None, "head", None),
        P("ctx", None, None),
        P("ctx", None, None),
        P("ctx", None, "head", None),
        P("ctx"),
    )
    out_specs = (P("ctx", None, "head", None), P("ctx", "head", None), P("ctx", "head", None))
    return jax.shard_map(on_device, mesh=mesh, in_specs=in_specs, out_specs=out_specs, check_vma=False)
```

```python
import functools

import jax
import jax.numpy as jnp
from jax import lax
from jax.experimental import pallas as pl
from jax.experimental.pallas import tpu as pltpu
from jax.sharding import PartitionSpec as P


WINDOW = 256
CHUNK = WINDOW // 2
PAD = 8
LOG2E = 1.4426950408889634
F32 = jnp.float32
BF16 = jnp.bfloat16
VMEM = pl.BlockSpec(memory_space=pltpu.VMEM)
SMEM = pl.BlockSpec(memory_space=pltpu.SMEM)
ANY = pl.BlockSpec(memory_space=pl.ANY)
HBM = pl.BlockSpec(memory_space=pltpu.HBM)
MIB = 1024 * 1024


def dot(a, b, contract):
    return lax.dot_general(a, b, (((contract[0],), (contract[1],)), ((), ())), preferred_element_type=F32)


def params(limit):
    return pltpu.CompilerParams(vmem_limit_bytes=limit * MIB)


def count_smaller(column, row):
    return jnp.sum((column < row).astype(F32), axis=0, keepdims=True)


def tail_kernel(sel_ref, key_ref, value_ref, docs_ref, kv_ref, halo_ref, buf, sem):
    half = halo_ref.shape[1]
    chunks = docs_ref.shape[0]
    first = key_ref.shape[0] - WINDOW
    copies = [
        pltpu.make_async_copy(ref.at[pl.ds(first, WINDOW)], buf.at[i], sem.at[i])
        for i, ref in enumerate((key_ref, value_ref))
    ]
    for copy in copies:
        copy.start()
    pad = jnp.zeros((PAD - 2, CHUNK), BF16)
    tail = jnp.concatenate([docs_ref[chunks - 2 :].astype(F32).astype(BF16), pad], 0)
    for i in range(2):
        copies[i].wait()
        kv_ref[i] = jnp.transpose(buf[i], (1, 0, 2))
        for h in range(half):
            halo_ref[i, h, :WINDOW] = kv_ref[i, sel_ref[0] * half + h]
            halo_ref[i, h, WINDOW:] = tail


def rest_kernel(sel_ref, key_ref, value_ref, docs_ref, tail_ref, kv_ref, halo_ref, low_ref, buf, sem, *, group):
    half = halo_ref.shape[1]
    chunks = docs_ref.shape[0]
    rest = kv_ref.shape[2]
    copies = [
        pltpu.make_async_copy(ref.at[pl.ds(0, rest)], buf.at[i], sem.at[i])
        for i, ref in enumerate((key_ref, value_ref))
    ]
    for copy in copies:
        copy.start()
    docs = docs_ref[...].astype(F32)
    columns = docs.T
    for c in range(chunks):
        row = docs[c : c + 1]
        count = sum(count_smaller(columns[:, b : b + 1], row) for b in range(c + 1))
        low = count.astype(jnp.int32) + (WINDOW - c * CHUNK)
        low_ref[c : c + 1, :] = jnp.concatenate([low] * group, 1)
    pad = jnp.zeros((PAD - 2, CHUNK), BF16)
    tail = jnp.concatenate([docs[chunks - 2 :].astype(BF16), pad], 0)
    for i in range(2):
        for h in range(half):
            halo_ref[i, h, :WINDOW] = tail_ref[i, sel_ref[1] * half + h]
            halo_ref[i, h, WINDOW:] = tail
    for i in range(2):
        copies[i].wait()
        kv_ref[i] = jnp.transpose(buf[i], (1, 0, 2))


def half_grads(items, get_query, get_keys, get_low, scale, group, put_dq, put_block):
    cols = CHUNK * group
    row = lax.broadcasted_iota(jnp.int32, (CHUNK, cols), 0)
    token = lax.broadcasted_iota(jnp.int32, (CHUNK, cols), 1) & (CHUNK - 1)
    old = row > token
    old_low = old.astype(F32).astype(BF16)
    new_low = 1 - old_low
    position = jnp.where(old, row, row + 2 * CHUNK)
    middle = row + CHUNK
    dqs, sums, state, left = {}, {}, {}, {}
    for c, h, _, _, keys in items:
        for b in range(3 * keys):
            left[h, c + b] = left.get((h, c + b), 0) + 1
    pending = {}
    for c, h, _, query, _ in items:
        pending[c] = pending.get(c, 0) + query

    def scores(item):
        c, h, source, _, _ = item
        q, do = get_query(c, h, source)
        k, v = get_keys(h, c)
        state[item] = (q, do, k, dot(k, q, (1, 1)), dot(v, do, (1, 1)))

    def soft(item):
        q, do, k, s, dp = state[item]
        low = get_low(item[0])
        s = [
            jnp.where(position >= low, jnp.where(old, s[:CHUNK], s[2 * CHUNK :]), -1e30),
            jnp.where(middle >= low, s[CHUNK : 2 * CHUNK], -1e30),
        ]
        dp = [jnp.where(old, dp[:CHUNK], dp[2 * CHUNK :]), dp[CHUNK : 2 * CHUNK]]
        top = functools.reduce(jnp.maximum, [jnp.max(x, axis=0, keepdims=True) for x in s])
        w = [jnp.exp2((x - top) * (scale * LOG2E)) for x in s]
        total = sum(jnp.sum(x, axis=0, keepdims=True) for x in w)
        inverse = 1.0 / total
        p = [x * inverse for x in w]
        delta = sum(jnp.sum(x * y, axis=0, keepdims=True) for x, y in zip(p, dp))
        ds = [(x * (y - delta)).astype(BF16) for x, y in zip(p, dp)]
        p = [x.astype(BF16) for x in p]
        p = jnp.concatenate([p[0] * old_low, p[1], p[0] * new_low], 0) if item[4] else None
        ds = jnp.concatenate([ds[0] * old_low, ds[1], ds[0] * new_low], 0)
        state[item] = (q, do, k, p, ds)

    def grads(item):
        c, h, _, query, keys = item
        q, do, k, p, ds = state.pop(item)
        if keys:
            dv = dot(p, do, (1, 0))
            dk = dot(ds, q, (1, 0))
        for b in range(3 * keys):
            rows = slice(b * CHUNK, (b + 1) * CHUNK)
            key = (h, c + b)
            new = (dk[rows], dv[rows])
            if key in sums:
                new = (sums[key][0] + new[0], sums[key][1] + new[1])
            sums[key] = new
            left[key] -= 1
            if not left[key]:
                put_block(h, c + b, *sums.pop(key))
        if query:
            dqs[c, h] = (dot(k.T, ds, (1, 0)) * scale).T.astype(BF16).reshape(group, CHUNK, -1)
            pending[c] -= 1
            if not pending[c]:
                heads = sorted(i for a, i in dqs if a == c)
                full = jnp.concatenate([dqs.pop((c, i)) for i in heads], 0)
                put_dq(c, jnp.transpose(full, (1, 0, 2)))

    scores(items[0])
    for n, item in enumerate(items):
        if n + 1 < len(items):
            scores(items[n + 1])
        if n:
            grads(items[n - 1])
        soft(item)
    grads(items[-1])


def store_rows(buf, sem, slot, dq_ref, rows, where):
    return pltpu.make_async_copy(buf.at[slot], dq_ref.at[rows, where, :], sem.at[slot])


def run_half(sel, chunks, items, group, half, q_ref, do_ref, get_keys, get_low, scale, put_block, dq_ref, buf, sem):
    rows = half * group
    where = pl.ds(pl.multiple_of(sel * rows, rows), rows)
    held = {}

    def tokens(c):
        return slice(chunks[c] * CHUNK, (chunks[c] + 1) * CHUNK)

    def get_query(c, h, source):
        if c not in held:
            held[c] = [jnp.transpose(ref[tokens(c), where, :], (1, 0, 2)) for ref in (q_ref, do_ref)]
        return [x[h * group : (h + 1) * group].reshape(group * CHUNK, -1) for x in held[c]]

    def put_dq(c, value):
        buf[c] = value
        store_rows(buf, sem, c, dq_ref, tokens(c), where).start()

    half_grads(items, get_query, get_keys, get_low, scale, group, put_dq, put_block)
    for c in range(len(chunks)):
        store_rows(buf, sem, c, dq_ref, tokens(c), where).wait()


def all_items(chunks, half):
    return [(c, h, 0, True, True) for c in range(len(chunks)) for h in range(half)]


def late_kernel(sel_ref, low_ref, q_ref, do_ref, rest_ref, tail_ref, *refs, chunks, group, n):
    dq_ref, part_ref, buf, sem = refs[-4:]
    half = part_ref.shape[1]
    scale = 1.0 / q_ref.shape[-1] ** 0.5
    sel = sel_ref[n]
    rest = rest_ref.shape[2]

    def get_keys(h, c):
        start, stop = (chunks[c] - 2) * CHUNK, (chunks[c] + 1) * CHUNK
        pieces = []
        for i in range(2):
            parts = []
            if start < rest:
                parts.append(rest_ref[i, sel * half + h, start : min(stop, rest)])
            if stop > rest:
                parts.append(tail_ref[i, sel * half + h, max(start - rest, 0) : stop - rest])
            pieces.append(jnp.concatenate(parts, 0))
        return pieces

    def put_block(h, b, dk, dv):
        block = slice((chunks[0] - 2 + b) * CHUNK, (chunks[0] - 1 + b) * CHUNK)
        part_ref[0, h, block] = dk * scale
        part_ref[1, h, block] = dv

    def get_low(c):
        return low_ref[chunks[c] : chunks[c] + 1, :]

    items = all_items(chunks, half)
    run_half(sel, chunks, items, group, half, q_ref, do_ref, get_keys, get_low, scale, put_block, dq_ref, buf, sem)


def early_kernel(sel_ref, docs_ref, low_ref, q_ref, do_ref, rest_ref, halo_ref, *refs, group, n, carry):
    part_ref = refs[0] if carry else None
    dq_ref, own_ref, back_ref, buf, sem = refs[-5:]
    half = own_ref.shape[1]
    scale = 1.0 / q_ref.shape[-1] ** 0.5
    sel = sel_ref[n]
    before = jnp.where(sel_ref[2] == 0, -1.0, halo_ref[0, 0, WINDOW:].astype(F32)).T
    lows = []
    for c in range(2):
        docs = docs_ref[c : c + 1, :].astype(F32)
        count = count_smaller(before[:, :1], docs) + count_smaller(before[:, 1:2], docs)
        count = jnp.concatenate([count] * group, 1)
        lows.append(low_ref[c : c + 1, :] - WINDOW + count.astype(jnp.int32))

    def get_keys(h, c):
        return [
            jnp.concatenate(
                [halo_ref[i, h, c * CHUNK : WINDOW], rest_ref[i, sel * half + h, : (c + 1) * CHUNK]], 0
            )
            for i in range(2)
        ]

    def put_block(h, b, dk, dv):
        dk = dk * scale
        if b < 2:
            block = slice(b * CHUNK, (b + 1) * CHUNK)
            back_ref[0, h, block] = dk.astype(BF16)
            back_ref[1, h, block] = dv.astype(BF16)
        else:
            block = slice((b - 2) * CHUNK, (b - 1) * CHUNK)
            if carry:
                dk, dv = dk + part_ref[0, h, block], dv + part_ref[1, h, block]
            own_ref[0, h, block] = dk.astype(own_ref.dtype)
            own_ref[1, h, block] = dv.astype(own_ref.dtype)

    items = all_items((0, 1), half)
    run_half(
        sel, (0, 1), items, group, half, q_ref, do_ref, get_keys, lambda c: lows[c], scale, put_block, dq_ref, buf, sem
    )


def finish_kernel(early_ref, first_in, part_ref, last_in, back_in, dk_ref, dv_ref):
    tokens = dk_ref.shape[0]
    for i, out in ((0, dk_ref), (1, dv_ref)):
        value = early_ref[i] + part_ref[i, :, :WINDOW] + first_in[i].astype(F32)
        out[:WINDOW] = jnp.transpose(value.astype(BF16), (1, 0, 2))
        late = part_ref[i, :, WINDOW:] + last_in[i].astype(F32)
        value = late[:, tokens - 2 * WINDOW :] + back_in[i].astype(F32)
        if tokens > 2 * WINDOW:
            value = jnp.concatenate([late[:, : tokens - 2 * WINDOW], value], 1)
        out[WINDOW:] = jnp.transpose(value.astype(BF16), (1, 0, 2))


def shift(block, axis, distance):
    devices = range(lax.axis_size(axis))
    return lax.ppermute(block, axis, [(i - distance, i) for i in devices if i - distance in devices])


def swap(block):
    return lax.ppermute(block, "head", [(0, 1), (1, 0)])


def on_device(queries, key_heads, value_heads, out_grad, doc_ids):
    tokens, kv_count, group, size = queries.shape
    half = kv_count // 2
    chunks = tokens // CHUNK
    shape = jax.ShapeDtypeStruct
    dma = pltpu.SemaphoreType.DMA
    head = lax.axis_index("head")
    sel = jnp.stack([1 - head, head, lax.axis_index("ctx")]).astype(jnp.int32)
    rows = queries.reshape(tokens, kv_count * group, size)
    grads = out_grad.reshape(tokens, kv_count * group, size)
    docs = doc_ids.reshape(chunks, CHUNK)
    key_heads = pltpu.with_memory_space_constraint(key_heads, pltpu.HBM)
    value_heads = pltpu.with_memory_space_constraint(value_heads, pltpu.HBM)
    halo_shape = shape((2, half, WINDOW + PAD, size), BF16)
    rest = tokens - WINDOW

    def cost(n):
        work = n * 10 * CHUNK * group * (WINDOW + CHUNK) * size
        return pl.CostEstimate(flops=work * 10, bytes_accessed=n * CHUNK * group * size * 8, transcendentals=0)

    def staging(n):
        return [pltpu.VMEM((n, CHUNK, half * group, size), BF16), dma((n,))]

    def call(body, operands, specs, out_specs, out_shape, scratch, limit, estimate=None, aliases=None):
        return pl.pallas_call(
            body,
            in_specs=specs,
            out_specs=out_specs,
            out_shape=out_shape,
            scratch_shapes=scratch,
            input_output_aliases=aliases or {},
            compiler_params=params(limit),
            cost_estimate=estimate,
        )(*operands)

    tail, halo_other = call(
        tail_kernel,
        (sel, key_heads, value_heads, docs),
        [SMEM, HBM, HBM, VMEM],
        [VMEM, VMEM],
        [shape((2, kv_count, WINDOW, size), BF16), halo_shape],
        [pltpu.VMEM((2, WINDOW, kv_count, size), BF16), dma((2,))],
        16,
    )
    halo_other = shift(halo_other, "ctx", 1)
    kv, halo_mine, low = call(
        functools.partial(rest_kernel, group=group),
        (sel, key_heads, value_heads, docs, tail),
        [SMEM, HBM, HBM, VMEM, VMEM],
        [VMEM] * 3,
        [shape((2, kv_count, rest, size), BF16), halo_shape, shape((chunks, CHUNK * group), jnp.int32)],
        [pltpu.VMEM((2, rest, kv_count, size), BF16), dma((2,))],
        16,
    )
    halo_mine = shift(halo_mine, "ctx", 1)
    late_chunks = tuple(range(2, chunks))
    part_shape = shape((2, half, tokens, size), F32)

    def late(n, query_grad):
        operands = [sel, low, rows, grads, kv, tail]
        specs = [SMEM] + [VMEM] * 5
        if query_grad is not None:
            operands.append(query_grad)
            specs.append(ANY)
        return call(
            functools.partial(late_kernel, chunks=late_chunks, group=group, n=n),
            operands,
            specs,
            [ANY, VMEM],
            [shape(rows.shape, BF16), part_shape],
            staging(len(late_chunks)),
            20,
            cost(half * len(late_chunks)),
            {len(operands) - 1: 0} if query_grad is not None else None,
        )

    def early(n, halo, part, query_grad, emit):
        operands = [sel, docs, low, rows, grads, kv, halo]
        if part is not None:
            operands.append(part)
        return call(
            functools.partial(early_kernel, group=group, n=n, carry=part is not None),
            operands + [query_grad],
            [SMEM] + [VMEM] * (len(operands) - 1) + [ANY],
            [ANY, VMEM, VMEM],
            [
                shape(rows.shape, BF16),
                shape((2, half, WINDOW, size), emit),
                shape((2, half, WINDOW, size), BF16),
            ],
            staging(2),
            20,
            cost(half * 2),
            {len(operands): 0},
        )

    query_grad, part_other = late(0, None)
    query_grad, first_other, back_other = early(0, halo_other, part_other, query_grad, BF16)
    back_other = shift(back_other, "ctx", -1)
    first_other = swap(first_other)
    query_grad, early_mine, back_mine = early(1, halo_mine, None, query_grad, F32)
    back_mine = shift(back_mine, "ctx", -1)
    last_other = part_other[:, :, WINDOW:]
    last_other = last_other.at[:, :, tokens - 2 * WINDOW :].add(back_other.astype(F32)).astype(BF16)
    last_other = swap(last_other)
    query_grad, part_mine = late(1, query_grad)
    out = shape((tokens, half, size), BF16)
    key_grad, value_grad = call(
        finish_kernel,
        (early_mine, first_other, part_mine, last_other, back_mine),
        [VMEM] * 5,
        [VMEM] * 2,
        [out, out],
        [],
        16,
    )
    return query_grad.reshape(queries.shape), key_grad, value_grad


def solution(mesh):
    in_specs = (
        P("ctx", None, "head", None),
        P("ctx", None, None),
        P("ctx", None, None),
        P("ctx", None, "head", None),
        P("ctx"),
    )
    out_specs = (P("ctx", None, "head", None), P("ctx", "head", None), P("ctx", "head", None))

    return jax.shard_map(on_device, mesh=mesh, in_specs=in_specs, out_specs=out_specs, check_vma=False)
```

```python
import functools

import jax
import jax.numpy as jnp
from jax import lax
from jax.experimental import pallas as pl
from jax.experimental.pallas import tpu as pltpu
from jax.sharding import PartitionSpec as P


WINDOW = 256
CHUNK = WINDOW // 2
PAD = 8
LOG2E = 1.4426950408889634
F32 = jnp.float32
BF16 = jnp.bfloat16
VMEM = pl.BlockSpec(memory_space=pltpu.VMEM)
SMEM = pl.BlockSpec(memory_space=pltpu.SMEM)
ANY = pl.BlockSpec(memory_space=pl.ANY)
HBM = pl.BlockSpec(memory_space=pltpu.HBM)
MIB = 1024 * 1024


def dot(a, b, contract):
    return lax.dot_general(a, b, (((contract[0],), (contract[1],)), ((), ())), preferred_element_type=F32)


def params(limit):
    return pltpu.CompilerParams(vmem_limit_bytes=limit * MIB)


def count_smaller(column, row):
    return jnp.sum((column < row).astype(F32), axis=0, keepdims=True)


def tail_kernel(sel_ref, key_ref, value_ref, docs_ref, kv_ref, halo_ref, buf, docs_buf, sem):
    half = halo_ref.shape[1]
    chunks = docs_ref.shape[0]
    first = key_ref.shape[0] - WINDOW
    copies = [
        pltpu.make_async_copy(ref.at[pl.ds(first, WINDOW)], buf.at[i], sem.at[i])
        for i, ref in enumerate((key_ref, value_ref))
    ]
    copies.append(pltpu.make_async_copy(docs_ref, docs_buf, sem.at[2]))
    for copy in copies:
        copy.start()
    copies[2].wait()
    pad = jnp.zeros((PAD - 2, CHUNK), BF16)
    tail = jnp.concatenate([docs_buf[chunks - 2 :].astype(F32).astype(BF16), pad], 0)
    for i in range(2):
        copies[i].wait()
        kv_ref[i] = jnp.transpose(buf[i], (1, 0, 2))
        for h in range(half):
            halo_ref[i, h, :WINDOW] = kv_ref[i, sel_ref[0] * half + h]
            halo_ref[i, h, WINDOW:] = tail


def rest_of_block(sel_ref, key_ref, value_ref, docs_ref, tail_ref, kv_ref, halo_ref, low_ref, group):
    half = halo_ref.shape[1]
    chunks = docs_ref.shape[0]
    rest = kv_ref.shape[2]
    docs = docs_ref[...].astype(F32)
    columns = docs.T
    for c in range(chunks):
        row = docs[c : c + 1]
        count = sum(count_smaller(columns[:, b : b + 1], row) for b in range(c + 1))
        low = count.astype(jnp.int32) + (WINDOW - c * CHUNK)
        low_ref[c : c + 1, :] = jnp.concatenate([low] * group, 1)
    for i, ref in enumerate((key_ref, value_ref)):
        kv_ref[i] = jnp.transpose(ref[:rest], (1, 0, 2))
    pad = jnp.zeros((PAD - 2, CHUNK), BF16)
    tail = jnp.concatenate([docs[chunks - 2 :].astype(BF16), pad], 0)
    for i in range(2):
        for h in range(half):
            halo_ref[i, h, :WINDOW] = tail_ref[i, sel_ref[1] * half + h]
            halo_ref[i, h, WINDOW:] = tail


def half_grads(items, get_query, get_keys, get_low, scale, group, put_dq, put_block):
    cols = CHUNK * group
    row = lax.broadcasted_iota(jnp.int32, (CHUNK, cols), 0)
    token = lax.broadcasted_iota(jnp.int32, (CHUNK, cols), 1) & (CHUNK - 1)
    old = row > token
    old_low = old.astype(F32).astype(BF16)
    new_low = 1 - old_low
    position = jnp.where(old, row, row + 2 * CHUNK)
    middle = row + CHUNK
    dqs, sums, state, left = {}, {}, {}, {}
    for c, h, _, _, keys in items:
        for b in range(3 * keys):
            left[h, c + b] = left.get((h, c + b), 0) + 1
    pending = {}
    for c, h, _, query, _ in items:
        pending[c] = pending.get(c, 0) + query

    def scores(item):
        c, h, source, _, _ = item
        q, do = get_query(c, h, source)
        k, v = get_keys(h, c)
        state[item] = (q, do, k, dot(k, q, (1, 1)), dot(v, do, (1, 1)))

    def soft(item):
        q, do, k, s, dp = state[item]
        low = get_low(item[0])
        s = [
            jnp.where(position >= low, jnp.where(old, s[:CHUNK], s[2 * CHUNK :]), -1e30),
            jnp.where(middle >= low, s[CHUNK : 2 * CHUNK], -1e30),
        ]
        dp = [jnp.where(old, dp[:CHUNK], dp[2 * CHUNK :]), dp[CHUNK : 2 * CHUNK]]
        top = functools.reduce(jnp.maximum, [jnp.max(x, axis=0, keepdims=True) for x in s])
        w = [jnp.exp2((x - top) * (scale * LOG2E)) for x in s]
        total = sum(jnp.sum(x, axis=0, keepdims=True) for x in w)
        inverse = 1.0 / total
        p = [x * inverse for x in w]
        delta = sum(jnp.sum(x * y, axis=0, keepdims=True) for x, y in zip(p, dp))
        ds = [(x * (y - delta)).astype(BF16) for x, y in zip(p, dp)]
        p = [x.astype(BF16) for x in p]
        p = jnp.concatenate([p[0] * old_low, p[1], p[0] * new_low], 0) if item[4] else None
        ds = jnp.concatenate([ds[0] * old_low, ds[1], ds[0] * new_low], 0)
        state[item] = (q, do, k, p, ds)

    def grads(item):
        c, h, _, query, keys = item
        q, do, k, p, ds = state.pop(item)
        if keys:
            dv = dot(p, do, (1, 0))
            dk = dot(ds, q, (1, 0))
        for b in range(3 * keys):
            rows = slice(b * CHUNK, (b + 1) * CHUNK)
            key = (h, c + b)
            new = (dk[rows], dv[rows])
            if key in sums:
                new = (sums[key][0] + new[0], sums[key][1] + new[1])
            sums[key] = new
            left[key] -= 1
            if not left[key]:
                put_block(h, c + b, *sums.pop(key))
        if query:
            dqs[c, h] = (dot(k.T, ds, (1, 0)) * scale).T.astype(BF16).reshape(group, CHUNK, -1)
            pending[c] -= 1
            if not pending[c]:
                heads = sorted(i for a, i in dqs if a == c)
                full = jnp.concatenate([dqs.pop((c, i)) for i in heads], 0)
                put_dq(c, jnp.transpose(full, (1, 0, 2)))

    scores(items[0])
    for n, item in enumerate(items):
        if n + 1 < len(items):
            scores(items[n + 1])
        if n:
            grads(items[n - 1])
        soft(item)
    grads(items[-1])


def store_rows(buf, sem, slot, dq_ref, rows, where):
    return pltpu.make_async_copy(buf.at[slot], dq_ref.at[rows, where, :], sem.at[slot])


def run_half(sel, chunks, items, group, half, q_ref, do_ref, get_keys, get_low, scale, put_block, dq_ref, buf, sem, fetch=None):
    rows = half * group
    where = pl.ds(pl.multiple_of(sel * rows, rows), rows)
    held = {}

    def tokens(c):
        return slice(chunks[c] * CHUNK, (chunks[c] + 1) * CHUNK)

    def get_query(c, h, source):
        if c not in held:
            read = fetch(c) if fetch else [ref[tokens(c), where, :] for ref in (q_ref, do_ref)]
            held[c] = [jnp.transpose(x, (1, 0, 2)) for x in read]
        return [x[h * group : (h + 1) * group].reshape(group * CHUNK, -1) for x in held[c]]

    def put_dq(c, value):
        buf[c] = value
        store_rows(buf, sem, c, dq_ref, tokens(c), where).start()

    half_grads(items, get_query, get_keys, get_low, scale, group, put_dq, put_block)
    for c in range(len(chunks)):
        store_rows(buf, sem, c, dq_ref, tokens(c), where).wait()


def all_items(chunks, half):
    return [(c, h, 0, True, True) for c in range(len(chunks)) for h in range(half)]


def run_late(sel, chunks, group, q_ref, do_ref, rest_ref, tail_ref, low_ref, dq_ref, part_ref, buf, sem, fetch=None):
    half = part_ref.shape[1]
    scale = 1.0 / q_ref.shape[-1] ** 0.5
    rest = rest_ref.shape[2]

    def get_keys(h, c):
        start, stop = (chunks[c] - 2) * CHUNK, (chunks[c] + 1) * CHUNK
        pieces = []
        for i in range(2):
            parts = []
            if start < rest:
                parts.append(rest_ref[i, sel * half + h, start : min(stop, rest)])
            if stop > rest:
                parts.append(tail_ref[i, sel * half + h, max(start - rest, 0) : stop - rest])
            pieces.append(jnp.concatenate(parts, 0))
        return pieces

    def put_block(h, b, dk, dv):
        block = slice((chunks[0] - 2 + b) * CHUNK, (chunks[0] - 1 + b) * CHUNK)
        part_ref[0, h, block] = dk * scale
        part_ref[1, h, block] = dv

    def get_low(c):
        return low_ref[chunks[c] : chunks[c] + 1, :]

    items = all_items(chunks, half)
    run_half(
        sel, chunks, items, group, half, q_ref, do_ref, get_keys, get_low, scale, put_block, dq_ref, buf, sem, fetch
    )


def first_kernel(
    sel_ref, docs_ref, key_ref, value_ref, tail_ref, q_ref, do_ref, *refs, chunks, group
):
    dq_ref, part_ref, kv_ref, halo_ref, low_ref, q_buf, q_sem, buf, sem = refs
    rows = part_ref.shape[1] * group
    where = pl.ds(pl.multiple_of(sel_ref[0] * rows, rows), rows)

    def load(c, i):
        tokens = pl.ds(chunks[c] * CHUNK, CHUNK)
        return pltpu.make_async_copy(
            (q_ref, do_ref)[i].at[tokens, where, :], q_buf.at[c, i], q_sem.at[c, i]
        )

    for c in range(len(chunks)):
        for i in range(2):
            load(c, i).start()
    rest_of_block(sel_ref, key_ref, value_ref, docs_ref, tail_ref, kv_ref, halo_ref, low_ref, group)

    def fetch(c):
        for i in range(2):
            load(c, i).wait()
        return q_buf[c, 0], q_buf[c, 1]

    run_late(
        sel_ref[0], chunks, group, q_ref, do_ref, kv_ref, tail_ref, low_ref, dq_ref, part_ref, buf, sem, fetch
    )


def late_kernel(sel_ref, low_ref, q_ref, do_ref, rest_ref, tail_ref, dq_in, dq_ref, part_ref, buf, sem, *, chunks, group):
    run_late(sel_ref[1], chunks, group, q_ref, do_ref, rest_ref, tail_ref, low_ref, dq_ref, part_ref, buf, sem)


def early_kernel(sel_ref, docs_ref, low_ref, q_ref, do_ref, rest_ref, halo_ref, *refs, group, n, carry):
    part_ref = refs[0] if carry else None
    dq_ref, own_ref, back_ref, buf, sem = refs[-5:]
    half = own_ref.shape[1]
    scale = 1.0 / q_ref.shape[-1] ** 0.5
    sel = sel_ref[n]
    before = jnp.where(sel_ref[2] == 0, -1.0, halo_ref[0, 0, WINDOW:].astype(F32)).T
    lows = []
    for c in range(2):
        docs = docs_ref[c : c + 1, :].astype(F32)
        count = count_smaller(before[:, :1], docs) + count_smaller(before[:, 1:2], docs)
        count = jnp.concatenate([count] * group, 1)
        lows.append(low_ref[c : c + 1, :] - WINDOW + count.astype(jnp.int32))

    def get_keys(h, c):
        return [
            jnp.concatenate(
                [halo_ref[i, h, c * CHUNK : WINDOW], rest_ref[i, sel * half + h, : (c + 1) * CHUNK]], 0
            )
            for i in range(2)
        ]

    def put_block(h, b, dk, dv):
        dk = dk * scale
        if b < 2:
            block = slice(b * CHUNK, (b + 1) * CHUNK)
            back_ref[0, h, block] = dk.astype(BF16)
            back_ref[1, h, block] = dv.astype(BF16)
        else:
            block = slice((b - 2) * CHUNK, (b - 1) * CHUNK)
            if carry:
                dk, dv = dk + part_ref[0, h, block], dv + part_ref[1, h, block]
            own_ref[0, h, block] = dk.astype(own_ref.dtype)
            own_ref[1, h, block] = dv.astype(own_ref.dtype)

    items = all_items((0, 1), half)
    run_half(
        sel, (0, 1), items, group, half, q_ref, do_ref, get_keys, lambda c: lows[c], scale, put_block, dq_ref, buf, sem
    )


def finish_kernel(early_ref, first_in, part_ref, last_in, back_in, dk_ref, dv_ref):
    tokens = dk_ref.shape[0]
    for i, out in ((0, dk_ref), (1, dv_ref)):
        value = early_ref[i] + part_ref[i, :, :WINDOW] + first_in[i].astype(F32)
        out[:WINDOW] = jnp.transpose(value.astype(BF16), (1, 0, 2))
        late = part_ref[i, :, WINDOW:] + last_in[i].astype(F32)
        value = late[:, tokens - 2 * WINDOW :] + back_in[i].astype(F32)
        if tokens > 2 * WINDOW:
            value = jnp.concatenate([late[:, : tokens - 2 * WINDOW], value], 1)
        out[WINDOW:] = jnp.transpose(value.astype(BF16), (1, 0, 2))


def shift(block, axis, distance):
    devices = range(lax.axis_size(axis))
    return lax.ppermute(block, axis, [(i - distance, i) for i in devices if i - distance in devices])


def swap(block):
    return lax.ppermute(block, "head", [(0, 1), (1, 0)])


def in_hbm(array):
    return pltpu.with_memory_space_constraint(array, pltpu.HBM)


def on_device(queries, key_heads, value_heads, out_grad, doc_ids):
    tokens, kv_count, group, size = queries.shape
    half = kv_count // 2
    chunks = tokens // CHUNK
    shape = jax.ShapeDtypeStruct
    dma = pltpu.SemaphoreType.DMA
    head = lax.axis_index("head")
    sel = jnp.stack([1 - head, head, lax.axis_index("ctx")]).astype(jnp.int32)
    rows = queries.reshape(tokens, kv_count * group, size)
    grads = out_grad.reshape(tokens, kv_count * group, size)
    docs = doc_ids.reshape(chunks, CHUNK)
    halo_shape = shape((2, half, WINDOW + PAD, size), BF16)
    rest = tokens - WINDOW

    def cost(n):
        work = n * 10 * CHUNK * group * (WINDOW + CHUNK) * size
        return pl.CostEstimate(flops=work * 10, bytes_accessed=n * CHUNK * group * size * 8, transcendentals=0)

    def staging(n):
        return [pltpu.VMEM((n, CHUNK, half * group, size), BF16), dma((n,))]

    def call(body, operands, specs, out_specs, out_shape, scratch, limit, estimate=None, aliases=None):
        return pl.pallas_call(
            body,
            in_specs=specs,
            out_specs=out_specs,
            out_shape=out_shape,
            scratch_shapes=scratch,
            input_output_aliases=aliases or {},
            compiler_params=params(limit),
            cost_estimate=estimate,
        )(*operands)

    tail, halo_other = call(
        tail_kernel,
        (sel, in_hbm(key_heads), in_hbm(value_heads), in_hbm(docs)),
        [SMEM, HBM, HBM, HBM],
        [VMEM, VMEM],
        [shape((2, kv_count, WINDOW, size), BF16), halo_shape],
        [pltpu.VMEM((2, WINDOW, kv_count, size), BF16), pltpu.VMEM(docs.shape, docs.dtype), dma((3,))],
        16,
    )
    halo_other = shift(halo_other, "ctx", 1)
    late_chunks = tuple(range(2, chunks))
    part_shape = shape((2, half, tokens, size), F32)
    query_grad, part_other, kv, halo_mine, low = call(
        functools.partial(first_kernel, chunks=late_chunks, group=group),
        (sel, docs, key_heads, value_heads, tail, in_hbm(rows), in_hbm(grads)),
        [SMEM] + [VMEM] * 4 + [HBM] * 2,
        [ANY] + [VMEM] * 4,
        [
            shape(rows.shape, BF16),
            part_shape,
            shape((2, kv_count, rest, size), BF16),
            halo_shape,
            shape((chunks, CHUNK * group), jnp.int32),
        ],
        [
            pltpu.VMEM((len(late_chunks), 2, CHUNK, half * group, size), BF16),
            dma((len(late_chunks), 2)),
        ]
        + staging(len(late_chunks)),
        20,
        cost(half * len(late_chunks)),
    )
    halo_mine = shift(halo_mine, "ctx", 1)

    def early(n, halo, part, query_grad, emit):
        operands = [sel, docs, low, rows, grads, kv, halo]
        if part is not None:
            operands.append(part)
        return call(
            functools.partial(early_kernel, group=group, n=n, carry=part is not None),
            operands + [query_grad],
            [SMEM] + [VMEM] * (len(operands) - 1) + [ANY],
            [ANY, VMEM, VMEM],
            [
                shape(rows.shape, BF16),
                shape((2, half, WINDOW, size), emit),
                shape((2, half, WINDOW, size), BF16),
            ],
            staging(2),
            20,
            cost(half * 2),
            {len(operands): 0},
        )

    query_grad, first_other, back_other = early(0, halo_other, part_other, query_grad, BF16)
    back_other = shift(back_other, "ctx", -1)
    first_other = swap(first_other)
    query_grad, early_mine, back_mine = early(1, halo_mine, None, query_grad, F32)
    back_mine = shift(back_mine, "ctx", -1)
    last_other = part_other[:, :, WINDOW:]
    last_other = last_other.at[:, :, tokens - 2 * WINDOW :].add(back_other.astype(F32)).astype(BF16)
    last_other = swap(last_other)
    query_grad, part_mine = call(
        functools.partial(late_kernel, chunks=late_chunks, group=group),
        (sel, low, rows, grads, kv, tail, query_grad),
        [SMEM] + [VMEM] * 5 + [ANY],
        [ANY, VMEM],
        [shape(rows.shape, BF16), part_shape],
        staging(len(late_chunks)),
        20,
        cost(half * len(late_chunks)),
        {6: 0},
    )
    out = shape((tokens, half, size), BF16)
    key_grad, value_grad = call(
        finish_kernel,
        (early_mine, first_other, part_mine, last_other, back_mine),
        [VMEM] * 5,
        [VMEM] * 2,
        [out, out],
        [],
        16,
    )
    return query_grad.reshape(queries.shape), key_grad, value_grad


def solution(mesh):
    in_specs = (
        P("ctx", None, "head", None),
        P("ctx", None, None),
        P("ctx", None, None),
        P("ctx", None, "head", None),
        P("ctx"),
    )
    out_specs = (P("ctx", None, "head", None), P("ctx", "head", None), P("ctx", "head", None))

    return jax.shard_map(on_device, mesh=mesh, in_specs=in_specs, out_specs=out_specs, check_vma=False)
```

```python
import functools

import jax
import jax.numpy as jnp
from jax import lax
from jax.experimental import pallas as pl
from jax.experimental.pallas import tpu as pltpu
from jax.sharding import PartitionSpec as P


WINDOW = 256
CHUNK = WINDOW // 2
PAD = 8
STEP = 32
LOG2E = 1.4426950408889634
F32 = jnp.float32
BF16 = jnp.bfloat16
VMEM = pl.BlockSpec(memory_space=pltpu.VMEM)
SMEM = pl.BlockSpec(memory_space=pltpu.SMEM)
ANY = pl.BlockSpec(memory_space=pl.ANY)
HBM = pl.BlockSpec(memory_space=pltpu.HBM)
MIB = 1024 * 1024


def dot(a, b, contract):
    return lax.dot_general(a, b, (((contract[0],), (contract[1],)), ((), ())), preferred_element_type=F32)


def params(limit):
    return pltpu.CompilerParams(vmem_limit_bytes=limit * MIB)


def count_smaller(column, row):
    return jnp.sum((column < row).astype(F32), axis=0, keepdims=True)


def to_heads(ref, out, i):
    for r in range(0, out.shape[2], STEP):
        out[i, :, r : r + STEP] = jnp.transpose(ref[r : r + STEP], (1, 0, 2))


def tail_kernel(sel_ref, key_ref, value_ref, docs_ref, kv_ref, halo_ref, buf, docs_buf, sem):
    half = halo_ref.shape[1]
    chunks = docs_ref.shape[0]
    first = key_ref.shape[0] - WINDOW
    copies = [
        pltpu.make_async_copy(ref.at[pl.ds(first, WINDOW)], buf.at[i], sem.at[i])
        for i, ref in enumerate((key_ref, value_ref))
    ]
    copies.append(pltpu.make_async_copy(docs_ref, docs_buf, sem.at[2]))
    for copy in copies:
        copy.start()
    copies[2].wait()
    pad = jnp.zeros((PAD - 2, CHUNK), BF16)
    tail = jnp.concatenate([docs_buf[chunks - 2 :].astype(F32).astype(BF16), pad], 0)
    for i in range(2):
        copies[i].wait()
        to_heads(buf.at[i], kv_ref, i)
        for h in range(half):
            halo_ref[i, h, :WINDOW] = kv_ref[i, sel_ref[0] * half + h]
            halo_ref[i, h, WINDOW:] = tail


def rest_of_block(sel_ref, key_ref, value_ref, docs_ref, tail_ref, kv_ref, halo_ref, low_ref, group):
    half = halo_ref.shape[1]
    chunks = docs_ref.shape[0]
    docs = docs_ref[...].astype(F32)
    columns = docs.T
    for c in range(chunks):
        row = docs[c : c + 1]
        count = sum(count_smaller(columns[:, b : b + 1], row) for b in range(c + 1))
        low = count.astype(jnp.int32) + (WINDOW - c * CHUNK)
        low_ref[c : c + 1, :] = jnp.concatenate([low] * group, 1)
    for i, ref in enumerate((key_ref, value_ref)):
        to_heads(ref, kv_ref, i)
    pad = jnp.zeros((PAD - 2, CHUNK), BF16)
    tail = jnp.concatenate([docs[chunks - 2 :].astype(BF16), pad], 0)
    for i in range(2):
        for h in range(half):
            halo_ref[i, h, :WINDOW] = tail_ref[i, sel_ref[1] * half + h]
            halo_ref[i, h, WINDOW:] = tail


def half_grads(items, get_query, get_keys, get_low, scale, group, put_dq, put_block):
    cols = CHUNK * group
    row = lax.broadcasted_iota(jnp.int32, (CHUNK, cols), 0)
    token = lax.broadcasted_iota(jnp.int32, (CHUNK, cols), 1) & (CHUNK - 1)
    old = row > token
    old_low = old.astype(F32).astype(BF16)
    new_low = 1 - old_low
    position = jnp.where(old, row, row + 2 * CHUNK)
    middle = row + CHUNK
    dqs, sums, state, left = {}, {}, {}, {}
    for c, h, _, _, keys in items:
        for b in range(3 * keys):
            left[h, c + b] = left.get((h, c + b), 0) + 1
    pending = {}
    for c, h, _, query, _ in items:
        pending[c] = pending.get(c, 0) + query

    def scores(item):
        c, h, source, _, _ = item
        q, do = get_query(c, h, source)
        k, v = get_keys(h, c)
        state[item] = (q, do, k, dot(k, q, (1, 1)), dot(v, do, (1, 1)))

    def soft(item):
        q, do, k, s, dp = state[item]
        low = get_low(item[0])
        s = [
            jnp.where(position >= low, jnp.where(old, s[:CHUNK], s[2 * CHUNK :]), -1e30),
            jnp.where(middle >= low, s[CHUNK : 2 * CHUNK], -1e30),
        ]
        dp = [jnp.where(old, dp[:CHUNK], dp[2 * CHUNK :]), dp[CHUNK : 2 * CHUNK]]
        top = functools.reduce(jnp.maximum, [jnp.max(x, axis=0, keepdims=True) for x in s])
        w = [jnp.exp2((x - top) * (scale * LOG2E)) for x in s]
        total = sum(jnp.sum(x, axis=0, keepdims=True) for x in w)
        inverse = 1.0 / total
        p = [x * inverse for x in w]
        delta = sum(jnp.sum(x * y, axis=0, keepdims=True) for x, y in zip(p, dp))
        ds = [(x * (y - delta)).astype(BF16) for x, y in zip(p, dp)]
        p = [x.astype(BF16) for x in p]
        p = jnp.concatenate([p[0] * old_low, p[1], p[0] * new_low], 0) if item[4] else None
        ds = jnp.concatenate([ds[0] * old_low, ds[1], ds[0] * new_low], 0)
        state[item] = (q, do, k, p, ds)

    def grads(item):
        c, h, _, query, keys = item
        q, do, k, p, ds = state.pop(item)
        if keys:
            dv = dot(p, do, (1, 0))
            dk = dot(ds, q, (1, 0))
        for b in range(3 * keys):
            rows = slice(b * CHUNK, (b + 1) * CHUNK)
            key = (h, c + b)
            new = (dk[rows], dv[rows])
            if key in sums:
                new = (sums[key][0] + new[0], sums[key][1] + new[1])
            sums[key] = new
            left[key] -= 1
            if not left[key]:
                put_block(h, c + b, *sums.pop(key))
        if query:
            dqs[c, h] = (dot(k.T, ds, (1, 0)) * scale).T.astype(BF16).reshape(group, CHUNK, -1)
            pending[c] -= 1
            if not pending[c]:
                heads = sorted(i for a, i in dqs if a == c)
                full = jnp.concatenate([dqs.pop((c, i)) for i in heads], 0)
                put_dq(c, jnp.transpose(full, (1, 0, 2)))

    scores(items[0])
    for n, item in enumerate(items):
        if n + 1 < len(items):
            scores(items[n + 1])
        if n:
            grads(items[n - 1])
        soft(item)
    grads(items[-1])


def store_rows(buf, sem, slot, dq_ref, rows, where):
    return pltpu.make_async_copy(buf.at[slot], dq_ref.at[rows, where, :], sem.at[slot])


def load_rows(q_ref, do_ref, dst, sem, sel, chunks, rows):
    where = pl.ds(pl.multiple_of(sel * rows, rows), rows)
    return [
        [
            pltpu.make_async_copy(
                ref.at[pl.ds(chunk * CHUNK, CHUNK), where, :], dst.at[c, i], sem.at[c, i]
            )
            for i, ref in enumerate((q_ref, do_ref))
        ]
        for c, chunk in enumerate(chunks)
    ]


def run_half(sel, chunks, items, group, half, read, get_keys, get_low, scale, put_block, dq_ref, buf, sem):
    rows = half * group
    where = pl.ds(pl.multiple_of(sel * rows, rows), rows)
    held = {}

    def tokens(c):
        return slice(chunks[c] * CHUNK, (chunks[c] + 1) * CHUNK)

    def get_query(c, h, source):
        if c not in held:
            held[c] = [jnp.transpose(x, (1, 0, 2)) for x in read(c)]
        return [x[h * group : (h + 1) * group].reshape(group * CHUNK, -1) for x in held[c]]

    def put_dq(c, value):
        buf[c] = value
        store_rows(buf, sem, c, dq_ref, tokens(c), where).start()

    half_grads(items, get_query, get_keys, get_low, scale, group, put_dq, put_block)
    for c in range(len(chunks)):
        store_rows(buf, sem, c, dq_ref, tokens(c), where).wait()


def all_items(chunks, half):
    return [(c, h, 0, True, True) for c in range(len(chunks)) for h in range(half)]


def run_late(sel, chunks, group, read, rest_ref, tail_ref, low_ref, dq_ref, part_ref, buf, sem):
    half = part_ref.shape[1]
    scale = 1.0 / part_ref.shape[-1] ** 0.5
    rest = rest_ref.shape[2]

    def get_keys(h, c):
        start, stop = (chunks[c] - 2) * CHUNK, (chunks[c] + 1) * CHUNK
        pieces = []
        for i in range(2):
            parts = []
            if start < rest:
                parts.append(rest_ref[i, sel * half + h, start : min(stop, rest)])
            if stop > rest:
                parts.append(tail_ref[i, sel * half + h, max(start - rest, 0) : stop - rest])
            pieces.append(jnp.concatenate(parts, 0))
        return pieces

    def put_block(h, b, dk, dv):
        block = slice((chunks[0] - 2 + b) * CHUNK, (chunks[0] - 1 + b) * CHUNK)
        part_ref[0, h, block] = dk * scale
        part_ref[1, h, block] = dv

    def get_low(c):
        return low_ref[chunks[c] : chunks[c] + 1, :]

    items = all_items(chunks, half)
    run_half(sel, chunks, items, group, half, read, get_keys, get_low, scale, put_block, dq_ref, buf, sem)


def first_kernel(sel_ref, docs_ref, key_ref, value_ref, tail_ref, q_ref, do_ref, *refs, chunks, group):
    dq_ref, part_ref, kv_ref, halo_ref, low_ref, next_ref, q_buf, q_sem, next_sem, buf, sem = refs
    rows = part_ref.shape[1] * group
    copies = load_rows(q_ref, do_ref, q_buf, q_sem, sel_ref[0], chunks, rows)
    ahead = load_rows(q_ref, do_ref, next_ref, next_sem, sel_ref[0], (0, 1), rows)
    for pair in copies + ahead:
        for copy in pair:
            copy.start()
    rest_of_block(sel_ref, key_ref, value_ref, docs_ref, tail_ref, kv_ref, halo_ref, low_ref, group)

    def read(c):
        for copy in copies[c]:
            copy.wait()
        return q_buf[c, 0], q_buf[c, 1]

    run_late(sel_ref[0], chunks, group, read, kv_ref, tail_ref, low_ref, dq_ref, part_ref, buf, sem)
    for pair in ahead:
        for copy in pair:
            copy.wait()


def late_kernel(sel_ref, low_ref, rest_ref, tail_ref, qd_ref, dq_in, dq_ref, part_ref, buf, sem, *, chunks, group):
    def read(c):
        return qd_ref[c, 0], qd_ref[c, 1]

    run_late(sel_ref[1], chunks, group, read, rest_ref, tail_ref, low_ref, dq_ref, part_ref, buf, sem)


def early_kernel(
    sel_ref, docs_ref, low_ref, q_ref, do_ref, rest_ref, halo_ref, qd_ref, *refs, group, n, carry, ahead
):
    part_ref = refs[0] if carry else None
    dq_ref, own_ref, back_ref, next_ref, next_sem, buf, sem = refs[-7:]
    half = own_ref.shape[1]
    copies = load_rows(q_ref, do_ref, next_ref, next_sem, sel_ref[1], ahead, half * group)
    for pair in copies:
        for copy in pair:
            copy.start()
    scale = 1.0 / own_ref.shape[-1] ** 0.5
    sel = sel_ref[n]
    before = jnp.where(sel_ref[2] == 0, -1.0, halo_ref[0, 0, WINDOW:].astype(F32)).T
    lows = []
    for c in range(2):
        docs = docs_ref[c : c + 1, :].astype(F32)
        count = count_smaller(before[:, :1], docs) + count_smaller(before[:, 1:2], docs)
        count = jnp.concatenate([count] * group, 1)
        lows.append(low_ref[c : c + 1, :] - WINDOW + count.astype(jnp.int32))

    def get_keys(h, c):
        return [
            jnp.concatenate(
                [halo_ref[i, h, c * CHUNK : WINDOW], rest_ref[i, sel * half + h, : (c + 1) * CHUNK]], 0
            )
            for i in range(2)
        ]

    def put_block(h, b, dk, dv):
        dk = dk * scale
        if b < 2:
            block = slice(b * CHUNK, (b + 1) * CHUNK)
            back_ref[0, h, block] = dk.astype(BF16)
            back_ref[1, h, block] = dv.astype(BF16)
        else:
            block = slice((b - 2) * CHUNK, (b - 1) * CHUNK)
            if carry:
                dk, dv = dk + part_ref[0, h, block], dv + part_ref[1, h, block]
            own_ref[0, h, block] = dk.astype(own_ref.dtype)
            own_ref[1, h, block] = dv.astype(own_ref.dtype)

    def read(c):
        return qd_ref[c, 0], qd_ref[c, 1]

    items = all_items((0, 1), half)
    run_half(
        sel, (0, 1), items, group, half, read, get_keys, lambda c: lows[c], scale, put_block, dq_ref, buf, sem
    )
    for pair in copies:
        for copy in pair:
            copy.wait()


def out_rows(buf, sem, i, out, rows):
    return pltpu.make_async_copy(buf.at[i], out.at[rows], sem.at[i])


def begin_kernel(early_ref, first_in, part_ref, back_in, dk_ref, dv_ref, late_ref, buf, sem):
    late = late_ref.shape[2]
    for i, out in ((0, dk_ref), (1, dv_ref)):
        for r in range(0, WINDOW, STEP):
            rows = slice(r, r + STEP)
            value = early_ref[i, :, rows] + part_ref[i, :, rows] + first_in[i, :, rows].astype(F32)
            buf[i, rows] = jnp.transpose(value.astype(BF16), (1, 0, 2))
        out_rows(buf, sem, i, out, pl.ds(0, WINDOW)).start()
        if late > WINDOW:
            late_ref[i, :, : late - WINDOW] = part_ref[i, :, WINDOW:late]
        late_ref[i, :, late - WINDOW :] = part_ref[i, :, late:] + back_in[i].astype(F32)
    for i, out in ((0, dk_ref), (1, dv_ref)):
        out_rows(buf, sem, i, out, pl.ds(0, WINDOW)).wait()


def finish_kernel(late_ref, last_in, dk_in, dv_in, dk_ref, dv_ref, buf, sem):
    late = late_ref.shape[2]
    for i, out in ((0, dk_ref), (1, dv_ref)):
        for r in range(0, late, STEP):
            rows = slice(r, r + STEP)
            value = late_ref[i, :, rows] + last_in[i, :, rows].astype(F32)
            buf[i, rows] = jnp.transpose(value.astype(BF16), (1, 0, 2))
        out_rows(buf, sem, i, out, pl.ds(WINDOW, late)).start()
    for i, out in ((0, dk_ref), (1, dv_ref)):
        out_rows(buf, sem, i, out, pl.ds(WINDOW, late)).wait()


def shift(block, axis, distance):
    devices = range(lax.axis_size(axis))
    return lax.ppermute(block, axis, [(i - distance, i) for i in devices if i - distance in devices])


def swap(block):
    return lax.ppermute(block, "head", [(0, 1), (1, 0)])


def in_hbm(array):
    return pltpu.with_memory_space_constraint(array, pltpu.HBM)


def on_device(queries, key_heads, value_heads, out_grad, doc_ids):
    tokens, kv_count, group, size = queries.shape
    half = kv_count // 2
    chunks = tokens // CHUNK
    shape = jax.ShapeDtypeStruct
    dma = pltpu.SemaphoreType.DMA
    head = lax.axis_index("head")
    sel = jnp.stack([1 - head, head, lax.axis_index("ctx")]).astype(jnp.int32)
    rows = queries.reshape(tokens, kv_count * group, size)
    grads = out_grad.reshape(tokens, kv_count * group, size)
    docs = doc_ids.reshape(chunks, CHUNK)
    halo_shape = shape((2, half, WINDOW + PAD, size), BF16)
    rest = tokens - WINDOW

    def cost(n):
        work = n * 10 * CHUNK * group * (WINDOW + CHUNK) * size
        return pl.CostEstimate(flops=work * 10, bytes_accessed=n * CHUNK * group * size * 8, transcendentals=0)

    def staging(n):
        return [pltpu.VMEM((n, CHUNK, half * group, size), BF16), dma((n,))]

    def call(body, operands, specs, out_specs, out_shape, scratch, limit, estimate=None, aliases=None):
        return pl.pallas_call(
            body,
            in_specs=specs,
            out_specs=out_specs,
            out_shape=out_shape,
            scratch_shapes=scratch,
            input_output_aliases=aliases or {},
            compiler_params=params(limit),
            cost_estimate=estimate,
        )(*operands)

    tail, halo_other = call(
        tail_kernel,
        (sel, in_hbm(key_heads), in_hbm(value_heads), in_hbm(docs)),
        [SMEM, HBM, HBM, HBM],
        [VMEM, VMEM],
        [shape((2, kv_count, WINDOW, size), BF16), halo_shape],
        [pltpu.VMEM((2, WINDOW, kv_count, size), BF16), pltpu.VMEM(docs.shape, docs.dtype), dma((3,))],
        16,
    )
    halo_other = shift(halo_other, "ctx", 1)
    late_chunks = tuple(range(2, chunks))
    part_shape = shape((2, half, tokens, size), F32)
    q_hbm, do_hbm = in_hbm(rows), in_hbm(grads)
    qd_shape = shape((2, 2, CHUNK, half * group, size), BF16)
    late_qd = shape((len(late_chunks),) + qd_shape.shape[1:], BF16)
    query_grad, part_other, kv, halo_mine, low, qd_other = call(
        functools.partial(first_kernel, chunks=late_chunks, group=group),
        (sel, docs, key_heads, value_heads, tail, q_hbm, do_hbm),
        [SMEM] + [VMEM] * 4 + [HBM] * 2,
        [ANY] + [VMEM] * 5,
        [
            shape(rows.shape, BF16),
            part_shape,
            shape((2, kv_count, rest, size), BF16),
            halo_shape,
            shape((chunks, CHUNK * group), jnp.int32),
            qd_shape,
        ],
        [pltpu.VMEM(late_qd.shape, BF16), dma((len(late_chunks), 2)), dma((2, 2))]
        + staging(len(late_chunks)),
        20,
        cost(half * len(late_chunks)),
    )
    halo_mine = shift(halo_mine, "ctx", 1)

    def early(n, halo, qd, part, query_grad, emit, ahead):
        operands = [sel, docs, low, q_hbm, do_hbm, kv, halo, qd]
        if part is not None:
            operands.append(part)
        return call(
            functools.partial(early_kernel, group=group, n=n, carry=part is not None, ahead=ahead),
            operands + [query_grad],
            [SMEM, VMEM, VMEM, HBM, HBM] + [VMEM] * (len(operands) - 5) + [ANY],
            [ANY, VMEM, VMEM, VMEM],
            [
                shape(rows.shape, BF16),
                shape((2, half, WINDOW, size), emit),
                shape((2, half, WINDOW, size), BF16),
                shape((len(ahead),) + qd_shape.shape[1:], BF16),
            ],
            [dma((len(ahead), 2))] + staging(2),
            20,
            cost(half * 2),
            {len(operands): 0},
        )

    query_grad, first_other, back_other, qd_mine = early(0, halo_other, qd_other, part_other, query_grad, BF16, (0, 1))
    back_other = shift(back_other, "ctx", -1)
    first_other = swap(first_other)
    query_grad, early_mine, back_mine, qd_late = early(1, halo_mine, qd_mine, None, query_grad, F32, late_chunks)
    back_mine = shift(back_mine, "ctx", -1)
    last_other = part_other[:, :, WINDOW:]
    last_other = last_other.at[:, :, tokens - 2 * WINDOW :].add(back_other.astype(F32)).astype(BF16)
    last_other = swap(last_other)
    query_grad, part_mine = call(
        functools.partial(late_kernel, chunks=late_chunks, group=group),
        (sel, low, kv, tail, qd_late, query_grad),
        [SMEM] + [VMEM] * 4 + [ANY],
        [ANY, VMEM],
        [shape(rows.shape, BF16), part_shape],
        staging(len(late_chunks)),
        20,
        cost(half * len(late_chunks)),
        {5: 0},
    )
    out = shape((tokens, half, size), BF16)
    late_tokens = tokens - WINDOW
    key_grad, value_grad, late_sum = call(
        begin_kernel,
        (early_mine, first_other, part_mine, back_mine),
        [VMEM] * 4,
        [ANY, ANY, VMEM],
        [out, out, shape((2, half, late_tokens, size), F32)],
        [pltpu.VMEM((2, WINDOW, half, size), BF16), dma((2,))],
        8,
    )
    key_grad, value_grad = call(
        finish_kernel,
        (late_sum, last_other, key_grad, value_grad),
        [VMEM, VMEM, ANY, ANY],
        [ANY, ANY],
        [out, out],
        [pltpu.VMEM((2, late_tokens, half, size), BF16), dma((2,))],
        8,
        aliases={2: 0, 3: 1},
    )
    return query_grad.reshape(queries.shape), key_grad, value_grad


def solution(mesh):
    in_specs = (
        P("ctx", None, "head", None),
        P("ctx", None, None),
        P("ctx", None, None),
        P("ctx", None, "head", None),
        P("ctx"),
    )
    out_specs = (P("ctx", None, "head", None), P("ctx", "head", None), P("ctx", "head", None))

    return jax.shard_map(on_device, mesh=mesh, in_specs=in_specs, out_specs=out_specs, check_vma=False)
```

```python
import functools

import jax
import jax.numpy as jnp
from jax import lax
from jax.experimental import pallas as pl
from jax.experimental.pallas import tpu as pltpu
from jax.sharding import PartitionSpec as P


WINDOW = 256
CHUNK = WINDOW // 2
PAD = 8
STEP = 32
MOVED = 1
LOG2E = 1.4426950408889634
F32 = jnp.float32
BF16 = jnp.bfloat16
VMEM = pl.BlockSpec(memory_space=pltpu.VMEM)
SMEM = pl.BlockSpec(memory_space=pltpu.SMEM)
ANY = pl.BlockSpec(memory_space=pl.ANY)
HBM = pl.BlockSpec(memory_space=pltpu.HBM)
MIB = 1024 * 1024


def dot(a, b, contract):
    return lax.dot_general(a, b, (((contract[0],), (contract[1],)), ((), ())), preferred_element_type=F32)


def params(limit):
    return pltpu.CompilerParams(vmem_limit_bytes=limit * MIB)


def count_smaller(column, row):
    return jnp.sum((column < row).astype(F32), axis=0, keepdims=True)


def to_heads(ref, out, i):
    for r in range(0, out.shape[2], STEP):
        out[i, :, r : r + STEP] = jnp.transpose(ref[r : r + STEP], (1, 0, 2))


def tail_kernel(
    sel_ref, key_ref, value_ref, docs_ref, q_ref, do_ref, kv_ref, halo_ref, raw_ref, lead_ref, buf, docs_buf, sem
):
    half = halo_ref.shape[1]
    chunks = docs_ref.shape[0]
    first = key_ref.shape[0] - WINDOW
    moved = pl.ds(sel_ref[0] * half + half - MOVED, MOVED)
    pairs = [(docs_ref, docs_buf)]
    pairs += [(ref.at[pl.ds(first, WINDOW)], buf.at[i]) for i, ref in enumerate((key_ref, value_ref))]
    pairs += [(ref.at[:, moved], lead_ref.at[i]) for i, ref in enumerate((q_ref, do_ref))]
    pairs += [(ref.at[pl.ds(0, first)], raw_ref.at[i]) for i, ref in enumerate((key_ref, value_ref))]
    copies = [pltpu.make_async_copy(*pair, sem.at[n]) for n, pair in enumerate(pairs)]
    for copy in copies:
        copy.start()
    copies[0].wait()
    pad = jnp.zeros((PAD - 2, CHUNK), BF16)
    tail = jnp.concatenate([docs_buf[chunks - 2 :].astype(F32).astype(BF16), pad], 0)
    for i in range(2):
        copies[1 + i].wait()
        to_heads(buf.at[i], kv_ref, i)
        for h in range(half):
            halo_ref[i, h, :WINDOW] = kv_ref[i, sel_ref[0] * half + h]
            halo_ref[i, h, WINDOW:] = tail
    for copy in copies[3:]:
        copy.wait()


def interleave(rows, group):
    shape = (rows.shape[1], rows.shape[1] * group)
    source = lax.div(lax.broadcasted_iota(jnp.int32, shape, 1), jnp.int32(group))
    pick = (lax.broadcasted_iota(jnp.int32, shape, 0) == source).astype(F32).astype(BF16)
    return dot(rows.astype(BF16), pick, (1, 0))


def rest_of_block(sel_ref, raw_ref, docs_ref, tail_ref, kv_ref, halo_ref, low_ref, group):
    half = halo_ref.shape[1]
    chunks = docs_ref.shape[0]
    docs = docs_ref[...].astype(F32)
    columns = docs.T
    counts = []
    for c in range(chunks):
        row = docs[c : c + 1]
        counts.append(sum(count_smaller(columns[:, b : b + 1], row) for b in range(c + 1)))
    counts = jnp.concatenate(counts, 0)
    coarse = jnp.floor(counts * (1.0 / CHUNK))
    split = interleave(jnp.concatenate([coarse, counts - coarse * CHUNK], 0), group)
    mixed = split[:chunks] * CHUNK + split[chunks:]
    base = WINDOW - CHUNK * lax.broadcasted_iota(jnp.int32, (chunks, CHUNK * group), 0)
    low_ref[0] = jnp.concatenate([counts] * group, 1).astype(jnp.int32) + base
    low_ref[1] = mixed.astype(jnp.int32) + base
    for i in range(2):
        to_heads(raw_ref.at[i], kv_ref, i)
    pad = jnp.zeros((PAD - 2, CHUNK), BF16)
    tail = jnp.concatenate([docs[chunks - 2 :].astype(BF16), pad], 0)
    for i in range(2):
        for h in range(half):
            halo_ref[i, h, :WINDOW] = tail_ref[i, sel_ref[1] * half + h]
            halo_ref[i, h, WINDOW:] = tail


def half_grads(items, get_query, get_keys, get_low, scale, group, put_dq, put_block):
    cols = CHUNK * group
    row = lax.broadcasted_iota(jnp.int32, (CHUNK, cols), 0)
    col = lax.broadcasted_iota(jnp.int32, (CHUNK, cols), 1)
    middle = row + CHUNK
    masks = {}
    for source in sorted({item[2] for item in items}):
        old = row > (lax.div(col, jnp.int32(group)) if source else col & (CHUNK - 1))
        old_low = old.astype(F32).astype(BF16)
        masks[source] = (old, jnp.where(old, row, row + 2 * CHUNK), old_low, 1 - old_low)
    dqs, sums, state, left = {}, {}, {}, {}
    for c, h, _, _, keys in items:
        for b in range(3 * keys):
            left[h, c + b] = left.get((h, c + b), 0) + 1
    pending = {}
    for c, h, _, query, _ in items:
        pending[c] = pending.get(c, 0) + query

    def scores(item):
        c, h, source, _, _ = item
        q, do = get_query(c, h, source)
        k, v = get_keys(h, c)
        state[item] = (q, do, k, dot(k, q, (1, 1)), dot(v, do, (1, 1)))

    def soft(item):
        q, do, k, s, dp = state[item]
        old, position, old_low, new_low = masks[item[2]]
        low = get_low(item[0], item[2])
        s = [
            jnp.where(position >= low, jnp.where(old, s[:CHUNK], s[2 * CHUNK :]), -1e30),
            jnp.where(middle >= low, s[CHUNK : 2 * CHUNK], -1e30),
        ]
        dp = [jnp.where(old, dp[:CHUNK], dp[2 * CHUNK :]), dp[CHUNK : 2 * CHUNK]]
        top = functools.reduce(jnp.maximum, [jnp.max(x, axis=0, keepdims=True) for x in s])
        w = [jnp.exp2((x - top) * (scale * LOG2E)) for x in s]
        total = sum(jnp.sum(x, axis=0, keepdims=True) for x in w)
        inverse = 1.0 / total
        p = [x * inverse for x in w]
        delta = sum(jnp.sum(x * y, axis=0, keepdims=True) for x, y in zip(p, dp))
        ds = [(x * (y - delta)).astype(BF16) for x, y in zip(p, dp)]
        p = [x.astype(BF16) for x in p]
        p = jnp.concatenate([p[0] * old_low, p[1], p[0] * new_low], 0) if item[4] else None
        ds = jnp.concatenate([ds[0] * old_low, ds[1], ds[0] * new_low], 0)
        state[item] = (q, do, k, p, ds)

    def grads(item):
        c, h, _, query, keys = item
        q, do, k, p, ds = state.pop(item)
        if keys:
            dv = dot(p, do, (1, 0))
            dk = dot(ds, q, (1, 0))
        for b in range(3 * keys):
            rows = slice(b * CHUNK, (b + 1) * CHUNK)
            key = (h, c + b)
            new = (dk[rows], dv[rows])
            if key in sums:
                new = (sums[key][0] + new[0], sums[key][1] + new[1])
            sums[key] = new
            left[key] -= 1
            if not left[key]:
                put_block(h, c + b, *sums.pop(key))
        if query:
            dqs[c, h] = (dot(k.T, ds, (1, 0)) * scale).T.astype(BF16).reshape(group, CHUNK, -1)
            pending[c] -= 1
            if not pending[c]:
                heads = sorted(i for a, i in dqs if a == c)
                full = jnp.concatenate([dqs.pop((c, i)) for i in heads], 0)
                put_dq(c, jnp.transpose(full, (1, 0, 2)))

    scores(items[0])
    for n, item in enumerate(items):
        if n + 1 < len(items):
            scores(items[n + 1])
        if n:
            grads(items[n - 1])
        soft(item)
    grads(items[-1])


def store_before(dq_ref, staged_ref, sem, sel, chunks, rows):
    where = pl.ds(pl.multiple_of(sel * rows, rows), rows)
    return [
        pltpu.make_async_copy(staged_ref.at[c], dq_ref.at[pl.ds(chunk * CHUNK, CHUNK), where, :], sem.at[c])
        for c, chunk in enumerate(chunks)
    ]


def run_half(sel, chunks, items, group, half, q_ref, do_ref, lead_ref, get_keys, get_low, put_block, staged_ref):
    rows = half * group
    size = q_ref.shape[-1]
    where = pl.ds(pl.multiple_of(sel * rows, rows), rows)
    held = {}

    def get_query(c, h, source):
        if source:
            columns = slice(chunks[c] * CHUNK * group, (chunks[c] + 1) * CHUNK * group)
            return lead_ref[0, columns], lead_ref[1, columns]
        if c not in held:
            tokens = slice(chunks[c] * CHUNK, (chunks[c] + 1) * CHUNK)
            held[c] = [jnp.transpose(ref[tokens, where, :], (1, 0, 2)) for ref in (q_ref, do_ref)]
        return [x[h * group : (h + 1) * group].reshape(group * CHUNK, size) for x in held[c]]

    def put_dq(c, value):
        staged_ref[c] = value

    half_grads(items, get_query, get_keys, get_low, 1.0 / size**0.5, group, put_dq, put_block)


def partner_items(chunks, half):
    return [(c, h, 0, True, h < half - MOVED) for c in range(len(chunks)) for h in range(half)]


def own_items(chunks, half):
    items = []
    for c in range(len(chunks)):
        items += [(c, h, 0, True, True) for h in range(half)]
        items += [(c, half - MOVED, 1, False, True)]
    return items


def run_late(sel, chunks, items, group, half, q_ref, do_ref, lead_ref, rest_ref, tail_ref, low_ref, staged_ref, part_ref):
    scale = 1.0 / part_ref.shape[-1] ** 0.5
    rest = rest_ref.shape[2]

    def get_keys(h, c):
        start, stop = (chunks[c] - 2) * CHUNK, (chunks[c] + 1) * CHUNK
        pieces = []
        for i in range(2):
            parts = []
            if start < rest:
                parts.append(rest_ref[i, sel * half + h, start : min(stop, rest)])
            if stop > rest:
                parts.append(tail_ref[i, sel * half + h, max(start - rest, 0) : stop - rest])
            pieces.append(jnp.concatenate(parts, 0))
        return pieces

    def put_block(h, b, dk, dv):
        block = slice((chunks[0] - 2 + b) * CHUNK, (chunks[0] - 1 + b) * CHUNK)
        part_ref[0, h, block] = dk * scale
        part_ref[1, h, block] = dv

    def get_low(c, source):
        return low_ref[source, chunks[c] : chunks[c] + 1, :]

    run_half(sel, chunks, items, group, half, q_ref, do_ref, lead_ref, get_keys, get_low, put_block, staged_ref)


def first_kernel(
    sel_ref, docs_ref, raw_ref, tail_ref, q_ref, do_ref, staged_ref, part_ref, kv_ref, halo_ref, low_ref, *, chunks, group
):
    half = halo_ref.shape[1]
    rest_of_block(sel_ref, raw_ref, docs_ref, tail_ref, kv_ref, halo_ref, low_ref, group)
    items = partner_items(chunks, half)
    run_late(
        sel_ref[0], chunks, items, group, half, q_ref, do_ref, None, kv_ref, tail_ref, low_ref, staged_ref, part_ref
    )


def late_kernel(
    sel_ref, low_ref, q_ref, do_ref, lead_ref, rest_ref, tail_ref, before_ref, dq_in, dq_ref, staged_ref, part_ref, sem,
    *, chunks, before, group
):
    half = part_ref.shape[1]
    copies = store_before(dq_ref, before_ref, sem, sel_ref[before[0]], before[1], half * group)
    for copy in copies:
        copy.start()
    items = own_items(chunks, half)
    run_late(
        sel_ref[1], chunks, items, group, half, q_ref, do_ref, lead_ref, rest_ref, tail_ref, low_ref, staged_ref, part_ref
    )
    for copy in copies:
        copy.wait()


def early_kernel(sel_ref, docs_ref, low_ref, q_ref, do_ref, rest_ref, halo_ref, before_ref, *refs, group, n, before):
    extra_ref = refs[0]
    dq_ref, staged_ref, own_ref, back_ref, sem = refs[-5:]
    half = halo_ref.shape[1]
    scale = 1.0 / own_ref.shape[-1] ** 0.5
    sel = sel_ref[n]
    copies = store_before(dq_ref, before_ref, sem, sel_ref[before[0]], before[1], half * group)
    for copy in copies:
        copy.start()
    ahead = jnp.where(sel_ref[2] == 0, -1.0, halo_ref[0, 0, WINDOW:].astype(F32)).T
    counts = []
    for c in range(2):
        docs = docs_ref[c : c + 1, :].astype(F32)
        counts += [count_smaller(ahead[:, b : b + 1], docs) for b in range(2)]
    lows = {}
    if n:
        mixed = interleave(jnp.concatenate(counts, 0), group)
    for c in range(2):
        count = jnp.concatenate([counts[2 * c] + counts[2 * c + 1]] * group, 1)
        lows[c, 0] = low_ref[0, c : c + 1, :] - WINDOW + count.astype(jnp.int32)
        if n:
            count = mixed[2 * c : 2 * c + 1] + mixed[2 * c + 1 : 2 * c + 2]
            lows[c, 1] = low_ref[1, c : c + 1, :] - WINDOW + count.astype(jnp.int32)

    def get_keys(h, c):
        return [
            jnp.concatenate(
                [halo_ref[i, h, c * CHUNK : WINDOW], rest_ref[i, sel * half + h, : (c + 1) * CHUNK]], 0
            )
            for i in range(2)
        ]

    def put_block(h, b, dk, dv):
        dk = dk * scale
        if b < 2:
            block = slice(b * CHUNK, (b + 1) * CHUNK)
            back_ref[0, h, block] = dk.astype(BF16)
            back_ref[1, h, block] = dv.astype(BF16)
        else:
            block = slice((b - 2) * CHUNK, (b - 1) * CHUNK)
            if not n:
                dk, dv = dk + extra_ref[0, h, block], dv + extra_ref[1, h, block]
            own_ref[0, h, block] = dk.astype(own_ref.dtype)
            own_ref[1, h, block] = dv.astype(own_ref.dtype)

    items = own_items((0, 1), half) if n else partner_items((0, 1), half)
    run_half(
        sel, (0, 1), items, group, half, q_ref, do_ref, extra_ref if n else None, get_keys,
        lambda c, source: lows[c, source], put_block, staged_ref
    )
    for copy in copies:
        copy.wait()


def out_rows(buf, sem, i, out, rows):
    return pltpu.make_async_copy(buf.at[i], out.at[rows], sem.at[i])


def begin_kernel(
    sel_ref, early_ref, first_in, part_ref, back_in, before_ref, dq_in, dk_ref, dv_ref, late_ref, dq_ref, buf, sem, dq_sem,
    *, before
):
    late = late_ref.shape[2]
    shared = first_in.shape[1]
    stores = store_before(dq_ref, before_ref, dq_sem, sel_ref[before[0]], before[1], before_ref.shape[2])
    for copy in stores:
        copy.start()
    for i, out in ((0, dk_ref), (1, dv_ref)):
        for r in range(0, WINDOW, STEP):
            rows = slice(r, r + STEP)
            value = early_ref[i, :, rows] + part_ref[i, :, rows]
            value = jnp.concatenate([value[:shared] + first_in[i, :, rows].astype(F32), value[shared:]], 0)
            buf[i, rows] = jnp.transpose(value.astype(BF16), (1, 0, 2))
        out_rows(buf, sem, i, out, pl.ds(0, WINDOW)).start()
        if late > WINDOW:
            late_ref[i, :, : late - WINDOW] = part_ref[i, :, WINDOW:late]
        late_ref[i, :, late - WINDOW :] = part_ref[i, :, late:] + back_in[i].astype(F32)
    for i, out in ((0, dk_ref), (1, dv_ref)):
        out_rows(buf, sem, i, out, pl.ds(0, WINDOW)).wait()
    for copy in stores:
        copy.wait()


def finish_kernel(late_ref, last_in, dk_in, dv_in, dk_ref, dv_ref, buf, sem):
    late = late_ref.shape[2]
    shared = last_in.shape[1]
    for i, out in ((0, dk_ref), (1, dv_ref)):
        for r in range(0, late, STEP):
            rows = slice(r, r + STEP)
            value = late_ref[i, :, rows]
            value = jnp.concatenate([value[:shared] + last_in[i, :, rows].astype(F32), value[shared:]], 0)
            buf[i, rows] = jnp.transpose(value.astype(BF16), (1, 0, 2))
        out_rows(buf, sem, i, out, pl.ds(WINDOW, late)).start()
    for i, out in ((0, dk_ref), (1, dv_ref)):
        out_rows(buf, sem, i, out, pl.ds(WINDOW, late)).wait()


def shift(block, axis, distance):
    devices = range(lax.axis_size(axis))
    return lax.ppermute(block, axis, [(i - distance, i) for i in devices if i - distance in devices])


def swap(block):
    return lax.ppermute(block, "head", [(0, 1), (1, 0)])


def in_hbm(array):
    return pltpu.with_memory_space_constraint(array, pltpu.HBM)


def on_device(queries, key_heads, value_heads, out_grad, doc_ids):
    tokens, kv_count, group, size = queries.shape
    half = kv_count // 2
    shared = half - MOVED
    chunks = tokens // CHUNK
    rest = tokens - WINDOW
    shape = jax.ShapeDtypeStruct
    dma = pltpu.SemaphoreType.DMA
    head = lax.axis_index("head")
    sel = jnp.stack([1 - head, head, lax.axis_index("ctx")]).astype(jnp.int32)
    rows = queries.reshape(tokens, kv_count * group, size)
    grads = out_grad.reshape(tokens, kv_count * group, size)
    docs = doc_ids.reshape(chunks, CHUNK)
    halo_shape = shape((2, half, WINDOW + PAD, size), BF16)
    early_chunks, late_chunks = (0, 1), tuple(range(2, chunks))

    def cost(n):
        work = n * 10 * CHUNK * group * (WINDOW + CHUNK) * size
        return pl.CostEstimate(flops=work * 10, bytes_accessed=n * CHUNK * group * size * 8, transcendentals=0)

    def staged(chunks):
        return shape((len(chunks), CHUNK, half * group, size), BF16)

    def call(body, operands, specs, out_specs, out_shape, scratch, limit, estimate=None, aliases=None):
        return pl.pallas_call(
            body,
            in_specs=specs,
            out_specs=out_specs,
            out_shape=out_shape,
            scratch_shapes=scratch,
            input_output_aliases=aliases or {},
            compiler_params=params(limit),
            cost_estimate=estimate,
        )(*operands)

    tail, halo_other, raw, lead = call(
        tail_kernel,
        (sel, in_hbm(key_heads), in_hbm(value_heads), in_hbm(docs), in_hbm(queries), in_hbm(out_grad)),
        [SMEM] + [HBM] * 5,
        [VMEM] * 4,
        [
            shape((2, kv_count, WINDOW, size), BF16),
            halo_shape,
            shape((2, rest, kv_count, size), BF16),
            shape((2, tokens, MOVED, group, size), BF16),
        ],
        [pltpu.VMEM((2, WINDOW, kv_count, size), BF16), pltpu.VMEM(docs.shape, docs.dtype), dma((7,))],
        16,
    )
    halo_other = shift(halo_other, "ctx", 1)
    lead = swap(lead).reshape(2, tokens * group, size)
    staged_dq, part_other, kv, halo_mine, low = call(
        functools.partial(first_kernel, chunks=late_chunks, group=group),
        (sel, docs, raw, tail, rows, grads),
        [SMEM] + [VMEM] * 5,
        [VMEM] * 5,
        [
            staged(late_chunks),
            shape((2, shared, tokens, size), F32),
            shape((2, kv_count, rest, size), BF16),
            halo_shape,
            shape((2, chunks, CHUNK * group), jnp.int32),
        ],
        [],
        20,
        cost(half * len(late_chunks)),
    )
    halo_mine = shift(halo_mine, "ctx", 1)

    def early(n, halo, extra, heads, staged_dq, query_grad, emit, before):
        operands = [sel, docs, low, rows, grads, kv, halo, staged_dq, extra]
        specs = [SMEM] + [VMEM] * 8
        aliases = {}
        if query_grad is not None:
            aliases = {len(operands): 0}
            operands.append(query_grad)
            specs.append(ANY)
        return call(
            functools.partial(early_kernel, group=group, n=n, before=before),
            operands,
            specs,
            [ANY, VMEM, VMEM, VMEM],
            [
                shape(rows.shape, BF16),
                staged(early_chunks),
                shape((2, heads, WINDOW, size), emit),
                shape((2, heads, WINDOW, size), BF16),
            ],
            [dma((len(before[1]),))],
            20,
            cost(half * 2),
            aliases,
        )

    query_grad, staged_dq, first_other, back_other = early(
        0, halo_other, part_other, shared, staged_dq, None, BF16, (0, late_chunks)
    )
    back_other = shift(back_other, "ctx", -1)
    first_other = swap(first_other)
    query_grad, staged_dq, early_mine, back_mine = early(
        1, halo_mine, lead, half, staged_dq, query_grad, F32, (0, early_chunks)
    )
    back_mine = shift(back_mine, "ctx", -1)
    last_other = part_other[:, :, WINDOW:]
    last_other = last_other.at[:, :, tokens - 2 * WINDOW :].add(back_other.astype(F32)).astype(BF16)
    last_other = swap(last_other)
    query_grad, staged_dq, part_mine = call(
        functools.partial(late_kernel, chunks=late_chunks, before=(1, early_chunks), group=group),
        (sel, low, rows, grads, lead, kv, tail, staged_dq, query_grad),
        [SMEM] + [VMEM] * 7 + [ANY],
        [ANY, VMEM, VMEM],
        [shape(rows.shape, BF16), staged(late_chunks), shape((2, half, tokens, size), F32)],
        [dma((len(early_chunks),))],
        20,
        cost(half * len(late_chunks)),
        {8: 0},
    )
    out = shape((tokens, half, size), BF16)
    key_grad, value_grad, late_sum, query_grad = call(
        functools.partial(begin_kernel, before=(1, late_chunks)),
        (sel, early_mine, first_other, part_mine, back_mine, staged_dq, query_grad),
        [SMEM] + [VMEM] * 5 + [ANY],
        [ANY, ANY, VMEM, ANY],
        [out, out, shape((2, half, rest, size), F32), shape(rows.shape, BF16)],
        [pltpu.VMEM((2, WINDOW, half, size), BF16), dma((2,)), dma((len(late_chunks),))],
        8,
        aliases={6: 3},
    )
    key_grad, value_grad = call(
        finish_kernel,
        (late_sum, last_other, key_grad, value_grad),
        [VMEM, VMEM, ANY, ANY],
        [ANY, ANY],
        [out, out],
        [pltpu.VMEM((2, rest, half, size), BF16), dma((2,))],
        8,
        aliases={2: 0, 3: 1},
    )
    return query_grad.reshape(queries.shape), key_grad, value_grad


def solution(mesh):
    in_specs = (
        P("ctx", None, "head", None),
        P("ctx", None, None),
        P("ctx", None, None),
        P("ctx", None, "head", None),
        P("ctx"),
    )
    out_specs = (P("ctx", None, "head", None), P("ctx", "head", None), P("ctx", "head", None))

    return jax.shard_map(on_device, mesh=mesh, in_specs=in_specs, out_specs=out_specs, check_vma=False)
```

```python
import functools

import jax
import jax.numpy as jnp
from jax import lax
from jax.experimental import pallas as pl
from jax.experimental.pallas import tpu as pltpu
from jax.sharding import PartitionSpec as P


WINDOW = 256
CHUNK = WINDOW // 2
PAD = 8
STEP = 32
MOVED = 1
LOG2E = 1.4426950408889634
F32 = jnp.float32
BF16 = jnp.bfloat16
VMEM = pl.BlockSpec(memory_space=pltpu.VMEM)
SMEM = pl.BlockSpec(memory_space=pltpu.SMEM)
ANY = pl.BlockSpec(memory_space=pl.ANY)
HBM = pl.BlockSpec(memory_space=pltpu.HBM)
MIB = 1024 * 1024


def dot(a, b, contract):
    return lax.dot_general(a, b, (((contract[0],), (contract[1],)), ((), ())), preferred_element_type=F32)


def params(limit):
    return pltpu.CompilerParams(vmem_limit_bytes=limit * MIB)


def count_smaller(column, row):
    return jnp.sum((column < row).astype(F32), axis=0, keepdims=True)


def to_heads(ref, out, i):
    for r in range(0, out.shape[2], STEP):
        out[i, :, r : r + STEP] = jnp.transpose(ref[r : r + STEP], (1, 0, 2))


def tail_kernel(
    sel_ref, key_ref, value_ref, docs_ref, q_ref, do_ref, kv_ref, other_ref, mine_ref, raw_ref, lead_ref, buf, docs_buf, sem
):
    half = key_ref.shape[1] // 2
    chunks = docs_ref.shape[0]
    first = key_ref.shape[0] - WINDOW
    moved = pl.ds(sel_ref[0] * half + half - MOVED, MOVED)
    pairs = [(docs_ref, docs_buf)]
    pairs += [(ref.at[pl.ds(first, WINDOW)], buf.at[i]) for i, ref in enumerate((key_ref, value_ref))]
    pairs += [(ref.at[:, moved], lead_ref.at[i]) for i, ref in enumerate((q_ref, do_ref))]
    pairs += [(ref.at[pl.ds(0, first)], raw_ref.at[i]) for i, ref in enumerate((key_ref, value_ref))]
    copies = [pltpu.make_async_copy(*pair, sem.at[n]) for n, pair in enumerate(pairs)]
    for copy in copies:
        copy.start()
    copies[0].wait()
    pad = jnp.zeros((PAD - 2, CHUNK), BF16)
    tail = jnp.concatenate([docs_buf[chunks - 2 :].astype(F32).astype(BF16), pad], 0)
    for i in range(2):
        copies[1 + i].wait()
        to_heads(buf.at[i], kv_ref, i)
        for h in range(half):
            out, slot = (other_ref, h) if h < half - MOVED else (mine_ref, h + MOVED)
            out[i, slot, :WINDOW] = kv_ref[i, sel_ref[0] * half + h]
            out[i, slot, WINDOW:] = tail
            mine_ref[i, h, :WINDOW] = kv_ref[i, sel_ref[1] * half + h]
            mine_ref[i, h, WINDOW:] = tail
    for copy in copies[3:]:
        copy.wait()


def interleave(rows, group):
    shape = (rows.shape[1], rows.shape[1] * group)
    source = lax.div(lax.broadcasted_iota(jnp.int32, shape, 1), jnp.int32(group))
    pick = (lax.broadcasted_iota(jnp.int32, shape, 0) == source).astype(F32).astype(BF16)
    return dot(rows.astype(BF16), pick, (1, 0))


def rest_of_block(raw_ref, docs_ref, kv_ref, low_ref, group):
    chunks = docs_ref.shape[0]
    docs = docs_ref[...].astype(F32)
    columns = docs.T
    counts = []
    for c in range(chunks):
        row = docs[c : c + 1]
        counts.append(sum(count_smaller(columns[:, b : b + 1], row) for b in range(c + 1)))
    counts = jnp.concatenate(counts, 0)
    coarse = jnp.floor(counts * (1.0 / CHUNK))
    split = interleave(jnp.concatenate([coarse, counts - coarse * CHUNK], 0), group)
    mixed = split[:chunks] * CHUNK + split[chunks:]
    base = WINDOW - CHUNK * lax.broadcasted_iota(jnp.int32, (chunks, CHUNK * group), 0)
    low_ref[0] = jnp.concatenate([counts] * group, 1).astype(jnp.int32) + base
    low_ref[1] = mixed.astype(jnp.int32) + base
    for i in range(2):
        to_heads(raw_ref.at[i], kv_ref, i)


def half_grads(items, get_query, get_keys, get_low, scale, group, put_dq, put_block):
    cols = CHUNK * group
    row = lax.broadcasted_iota(jnp.int32, (CHUNK, cols), 0)
    col = lax.broadcasted_iota(jnp.int32, (CHUNK, cols), 1)
    middle = row + CHUNK
    masks = {}
    for source in sorted({item[2] for item in items}):
        old = row > (lax.div(col, jnp.int32(group)) if source else col & (CHUNK - 1))
        old_low = old.astype(F32).astype(BF16)
        masks[source] = (old, jnp.where(old, row, row + 2 * CHUNK), old_low, 1 - old_low)
    dqs, sums, state, left = {}, {}, {}, {}
    for c, h, _, _, keys in items:
        for b in range(3 * keys):
            left[h, c + b] = left.get((h, c + b), 0) + 1
    pending = {}
    for c, h, _, query, _ in items:
        pending[c] = pending.get(c, 0) + query

    def scores(item):
        c, h, source, _, _ = item
        q, do = get_query(c, h, source)
        k, v = get_keys(h, c)
        state[item] = (q, do, k, dot(k, q, (1, 1)), dot(v, do, (1, 1)))

    def soft(item):
        q, do, k, s, dp = state[item]
        old, position, old_low, new_low = masks[item[2]]
        low = get_low(item[0], item[2])
        s = [
            jnp.where(position >= low, jnp.where(old, s[:CHUNK], s[2 * CHUNK :]), -1e30),
            jnp.where(middle >= low, s[CHUNK : 2 * CHUNK], -1e30),
        ]
        dp = [jnp.where(old, dp[:CHUNK], dp[2 * CHUNK :]), dp[CHUNK : 2 * CHUNK]]
        top = functools.reduce(jnp.maximum, [jnp.max(x, axis=0, keepdims=True) for x in s])
        w = [jnp.exp2((x - top) * (scale * LOG2E)) for x in s]
        total = sum(jnp.sum(x, axis=0, keepdims=True) for x in w)
        inverse = 1.0 / total
        p = [x * inverse for x in w]
        delta = sum(jnp.sum(x * y, axis=0, keepdims=True) for x, y in zip(p, dp))
        ds = [(x * (y - delta)).astype(BF16) for x, y in zip(p, dp)]
        p = [x.astype(BF16) for x in p]
        p = jnp.concatenate([p[0] * old_low, p[1], p[0] * new_low], 0) if item[4] else None
        ds = jnp.concatenate([ds[0] * old_low, ds[1], ds[0] * new_low], 0)
        state[item] = (q, do, k, p, ds)

    def grads(item):
        c, h, _, query, keys = item
        q, do, k, p, ds = state.pop(item)
        if keys:
            dv = dot(p, do, (1, 0))
            dk = dot(ds, q, (1, 0))
        for b in range(3 * keys):
            rows = slice(b * CHUNK, (b + 1) * CHUNK)
            key = (h, c + b)
            new = (dk[rows], dv[rows])
            if key in sums:
                new = (sums[key][0] + new[0], sums[key][1] + new[1])
            sums[key] = new
            left[key] -= 1
            if not left[key]:
                put_block(h, c + b, *sums.pop(key))
        if query:
            dqs[c, h] = (dot(k.T, ds, (1, 0)) * scale).T.astype(BF16).reshape(group, CHUNK, -1)
            pending[c] -= 1
            if not pending[c]:
                heads = sorted(i for a, i in dqs if a == c)
                put_dq(c, jnp.concatenate([dqs.pop((c, i)) for i in heads], 0))

    scores(items[0])
    for n, item in enumerate(items):
        if n + 1 < len(items):
            scores(items[n + 1])
        if n:
            grads(items[n - 1])
        soft(item)
    grads(items[-1])


def store_before(dq_ref, staged_ref, sem, first, sel, chunks, rows):
    where = pl.ds(pl.multiple_of(sel * rows, rows), rows)
    return [
        pltpu.make_async_copy(
            staged_ref.at[c], dq_ref.at[pl.ds(chunk * CHUNK, CHUNK), where, :], sem.at[first + c]
        )
        for c, chunk in enumerate(chunks)
    ]


def run_half(sel, chunks, items, group, half, q_ref, do_ref, lead_ref, get_keys, get_low, put_block, staged_ref):
    rows = half * group
    size = q_ref.shape[-1]
    where = pl.ds(pl.multiple_of(sel * rows, rows), rows)
    held = {}

    def get_query(c, h, source):
        if source:
            columns = slice(chunks[c] * CHUNK * group, (chunks[c] + 1) * CHUNK * group)
            return lead_ref[0, columns], lead_ref[1, columns]
        if c not in held:
            tokens = slice(chunks[c] * CHUNK, (chunks[c] + 1) * CHUNK)
            held[c] = [jnp.transpose(ref[tokens, where, :], (1, 0, 2)) for ref in (q_ref, do_ref)]
        return [x[h * group : (h + 1) * group].reshape(group * CHUNK, size) for x in held[c]]

    def put_dq(c, value):
        staged_ref[c] = jnp.transpose(value, (1, 0, 2)) if value.shape[0] == rows else value

    half_grads(items, get_query, get_keys, get_low, 1.0 / size**0.5, group, put_dq, put_block)


def partner_items(chunks, half):
    return [(c, h, 0, True, True) for c in range(len(chunks)) for h in range(half - MOVED)]


def own_items(chunks, half):
    items = []
    for c in range(len(chunks)):
        items += [(c, h, 0, True, True) for h in range(half)]
        items += [(c, half - MOVED, 1, False, True)]
    return items


def block_keys(rest_ref, tail_ref, head, chunk):
    rest = rest_ref.shape[2]
    start, stop = (chunk - 2) * CHUNK, (chunk + 1) * CHUNK
    pieces = []
    for i in range(2):
        parts = []
        if start < rest:
            parts.append(rest_ref[i, head, start : min(stop, rest)])
        if stop > rest:
            parts.append(tail_ref[i, head, max(start - rest, 0) : stop - rest])
        pieces.append(jnp.concatenate(parts, 0))
    return pieces


def halo_keys(halo_ref, rest_ref, slot, head, chunk):
    return [
        jnp.concatenate([halo_ref[i, slot, chunk * CHUNK :WINDOW], rest_ref[i, head, : (chunk + 1) * CHUNK]], 0)
        for i in range(2)
    ]


def early_lows(sel_ref, docs_ref, low_ref, halo_ref, group, mixed):
    ahead = jnp.where(sel_ref[2] == 0, -1.0, halo_ref[0, 0, WINDOW:].astype(F32)).T
    counts = []
    for c in range(2):
        docs = docs_ref[c : c + 1, :].astype(F32)
        counts += [count_smaller(ahead[:, b : b + 1], docs) for b in range(2)]
    lows = {}
    if mixed:
        spread = interleave(jnp.concatenate(counts, 0), group)
    for c in range(2):
        count = jnp.concatenate([counts[2 * c] + counts[2 * c + 1]] * group, 1)
        lows[c, 0] = low_ref[0, c : c + 1, :] - WINDOW + count.astype(jnp.int32)
        if mixed:
            count = spread[2 * c : 2 * c + 1] + spread[2 * c + 1 : 2 * c + 2]
            lows[c, 1] = low_ref[1, c : c + 1, :] - WINDOW + count.astype(jnp.int32)
    return lows


def run_late(sel, chunks, items, group, half, q_ref, do_ref, lead_ref, rest_ref, tail_ref, low_ref, staged_ref, part_ref):
    scale = 1.0 / part_ref.shape[-1] ** 0.5

    def get_keys(h, c):
        return block_keys(rest_ref, tail_ref, sel * half + h, chunks[c])

    def put_block(h, b, dk, dv):
        block = slice((chunks[0] - 2 + b) * CHUNK, (chunks[0] - 1 + b) * CHUNK)
        part_ref[0, h, block] = dk * scale
        part_ref[1, h, block] = dv

    def get_low(c, source):
        return low_ref[source, chunks[c] : chunks[c] + 1, :]

    run_half(sel, chunks, items, group, half, q_ref, do_ref, lead_ref, get_keys, get_low, put_block, staged_ref)


def first_kernel(
    sel_ref, docs_ref, raw_ref, tail_ref, q_ref, do_ref, staged_ref, part_ref, kv_ref, low_ref, *, chunks, group
):
    half = kv_ref.shape[1] // 2
    rest_of_block(raw_ref, docs_ref, kv_ref, low_ref, group)
    items = partner_items(chunks, half)
    run_late(
        sel_ref[0], chunks, items, group, half, q_ref, do_ref, None, kv_ref, tail_ref, low_ref, staged_ref, part_ref
    )


def late_kernel(
    sel_ref, low_ref, q_ref, do_ref, lead_ref, rest_ref, tail_ref, staged_ref, part_ref, *, chunks, group
):
    half = part_ref.shape[1]
    items = own_items(chunks, half)
    run_late(
        sel_ref[1], chunks, items, group, half, q_ref, do_ref, lead_ref, rest_ref, tail_ref, low_ref, staged_ref, part_ref
    )


def moved_kernel(
    sel_ref, docs_ref, low_ref, q_ref, do_ref, rest_ref, tail_ref, halo_ref, own_early_ref, own_late_ref, early_ref, late_ref,
    dq_ref, buf, sem, *, chunks, group
):
    half = halo_ref.shape[1] - MOVED
    rows = half * group
    size = q_ref.shape[-1]
    early = own_early_ref.shape[0]
    total = early + len(chunks)
    copies = store_before(dq_ref, own_early_ref, sem, 0, sel_ref[1], range(early), rows)
    copies += store_before(dq_ref, own_late_ref, sem, early, sel_ref[1], chunks, rows)
    for copy in copies:
        copy.start()
    where = pl.ds(pl.multiple_of(sel_ref[0] * rows, rows), rows)
    head = sel_ref[0] * half + half - MOVED
    lows = early_lows(sel_ref, docs_ref, low_ref, halo_ref, group, False)

    def store(c):
        target = dq_ref.at[pl.ds(c * CHUNK, CHUNK), where, :]
        return pltpu.make_async_copy(buf.at[c], target, sem.at[total + c])

    def get_query(c, h, source):
        tokens = slice(c * CHUNK, (c + 1) * CHUNK)
        both = [jnp.transpose(ref[tokens, where, :], (1, 0, 2)) for ref in (q_ref, do_ref)]
        return [x[rows - MOVED * group :].reshape(group * CHUNK, size) for x in both]

    def get_keys(h, c):
        return halo_keys(halo_ref, rest_ref, half, head, c) if c < early else block_keys(rest_ref, tail_ref, head, c)

    def get_low(c, source):
        return lows[c, 0] if c < early else low_ref[0, c : c + 1, :]

    def put_dq(c, value):
        others = early_ref[c] if c < early else late_ref[c - early]
        buf[c] = jnp.transpose(jnp.concatenate([others, value], 0), (1, 0, 2))
        store(c).start()

    items = [(c, 0, 0, True, False) for c in range(total)]
    half_grads(items, get_query, get_keys, get_low, 1.0 / size**0.5, group, put_dq, None)
    for copy in copies:
        copy.wait()
    for c in range(total):
        store(c).wait()


def early_kernel(
    sel_ref, docs_ref, low_ref, q_ref, do_ref, rest_ref, halo_ref, extra_ref, staged_ref, own_ref, back_ref, *, group, n
):
    half = rest_ref.shape[1] // 2
    scale = 1.0 / own_ref.shape[-1] ** 0.5
    sel = sel_ref[n]
    lows = early_lows(sel_ref, docs_ref, low_ref, halo_ref, group, n > 0)

    def get_keys(h, c):
        return halo_keys(halo_ref, rest_ref, h, sel * half + h, c)

    def put_block(h, b, dk, dv):
        dk = dk * scale
        if b < 2:
            block = slice(b * CHUNK, (b + 1) * CHUNK)
            back_ref[0, h, block] = dk.astype(BF16)
            back_ref[1, h, block] = dv.astype(BF16)
        else:
            block = slice((b - 2) * CHUNK, (b - 1) * CHUNK)
            if not n:
                dk, dv = dk + extra_ref[0, h, block], dv + extra_ref[1, h, block]
            own_ref[0, h, block] = dk.astype(own_ref.dtype)
            own_ref[1, h, block] = dv.astype(own_ref.dtype)

    items = own_items((0, 1), half) if n else partner_items((0, 1), half)
    run_half(
        sel, (0, 1), items, group, half, q_ref, do_ref, extra_ref if n else None, get_keys,
        lambda c, source: lows[c, source], put_block, staged_ref
    )


def out_rows(buf, sem, i, out, rows):
    return pltpu.make_async_copy(buf.at[i], out.at[rows], sem.at[i])


def begin_kernel(early_ref, first_in, part_ref, dk_ref, dv_ref, buf, sem):
    shared = first_in.shape[1]
    for i, out in ((0, dk_ref), (1, dv_ref)):
        for r in range(0, WINDOW, STEP):
            rows = slice(r, r + STEP)
            value = early_ref[i, :, rows] + part_ref[i, :, rows]
            value = jnp.concatenate([value[:shared] + first_in[i, :, rows].astype(F32), value[shared:]], 0)
            buf[i, rows] = jnp.transpose(value.astype(BF16), (1, 0, 2))
        out_rows(buf, sem, i, out, pl.ds(0, WINDOW)).start()
    for i, out in ((0, dk_ref), (1, dv_ref)):
        out_rows(buf, sem, i, out, pl.ds(0, WINDOW)).wait()


def finish_kernel(part_ref, last_in, back_in, dk_in, dv_in, dk_ref, dv_ref, buf, sem):
    late = part_ref.shape[2] - WINDOW
    shared = last_in.shape[1]
    for i, out in ((0, dk_ref), (1, dv_ref)):
        for r in range(0, late, STEP):
            rows = slice(r, r + STEP)
            value = part_ref[i, :, WINDOW + r : WINDOW + r + STEP]
            skip = late - WINDOW
            if r >= skip:
                value = value + back_in[i, :, r - skip : r - skip + STEP].astype(F32)
            value = jnp.concatenate([value[:shared] + last_in[i, :, rows].astype(F32), value[shared:]], 0)
            buf[i, rows] = jnp.transpose(value.astype(BF16), (1, 0, 2))
        out_rows(buf, sem, i, out, pl.ds(WINDOW, late)).start()
    for i, out in ((0, dk_ref), (1, dv_ref)):
        out_rows(buf, sem, i, out, pl.ds(WINDOW, late)).wait()


def shift(block, axis, distance):
    devices = range(lax.axis_size(axis))
    return lax.ppermute(block, axis, [(i - distance, i) for i in devices if i - distance in devices])


def swap(block):
    return lax.ppermute(block, "head", [(0, 1), (1, 0)])


def in_hbm(array):
    return pltpu.with_memory_space_constraint(array, pltpu.HBM)


def on_device(queries, key_heads, value_heads, out_grad, doc_ids):
    tokens, kv_count, group, size = queries.shape
    half = kv_count // 2
    shared = half - MOVED
    chunks = tokens // CHUNK
    rest = tokens - WINDOW
    shape = jax.ShapeDtypeStruct
    dma = pltpu.SemaphoreType.DMA
    head = lax.axis_index("head")
    sel = jnp.stack([1 - head, head, lax.axis_index("ctx")]).astype(jnp.int32)
    rows = queries.reshape(tokens, kv_count * group, size)
    grads = out_grad.reshape(tokens, kv_count * group, size)
    docs = doc_ids.reshape(chunks, CHUNK)

    def halo_shape(heads):
        return shape((2, heads, WINDOW + PAD, size), BF16)

    early_chunks, late_chunks = (0, 1), tuple(range(2, chunks))

    def cost(n):
        work = n * 10 * CHUNK * group * (WINDOW + CHUNK) * size
        return pl.CostEstimate(flops=work * 10, bytes_accessed=n * CHUNK * group * size * 8, transcendentals=0)

    def staged(chunks):
        return shape((len(chunks), CHUNK, half * group, size), BF16)

    def by_head(chunks):
        return shape((len(chunks), shared * group, CHUNK, size), BF16)

    def call(body, operands, specs, out_specs, out_shape, scratch, limit, estimate=None, aliases=None):
        return pl.pallas_call(
            body,
            in_specs=specs,
            out_specs=out_specs,
            out_shape=out_shape,
            scratch_shapes=scratch,
            input_output_aliases=aliases or {},
            compiler_params=params(limit),
            cost_estimate=estimate,
        )(*operands)

    tail, halo_other, halo_mine, raw, lead = call(
        tail_kernel,
        (sel, in_hbm(key_heads), in_hbm(value_heads), in_hbm(docs), in_hbm(queries), in_hbm(out_grad)),
        [SMEM] + [HBM] * 5,
        [VMEM] * 5,
        [
            shape((2, kv_count, WINDOW, size), BF16),
            halo_shape(shared),
            halo_shape(half + MOVED),
            shape((2, rest, kv_count, size), BF16),
            shape((2, tokens, MOVED, group, size), BF16),
        ],
        [pltpu.VMEM((2, WINDOW, kv_count, size), BF16), pltpu.VMEM(docs.shape, docs.dtype), dma((7,))],
        16,
    )
    halo_other = shift(halo_other, "ctx", 1)
    halo_mine = shift(halo_mine, "ctx", 1)
    lead = swap(lead).reshape(2, tokens * group, size)
    late_dq, part_other, kv, low = call(
        functools.partial(first_kernel, chunks=late_chunks, group=group),
        (sel, docs, raw, tail, rows, grads),
        [SMEM] + [VMEM] * 5,
        [VMEM] * 4,
        [
            by_head(late_chunks),
            shape((2, shared, tokens, size), F32),
            shape((2, kv_count, rest, size), BF16),
            shape((2, chunks, CHUNK * group), jnp.int32),
        ],
        [],
        20,
        cost(half * len(late_chunks)),
    )

    def early(n, halo, extra, heads, staged_dq, emit):
        return call(
            functools.partial(early_kernel, group=group, n=n),
            (sel, docs, low, rows, grads, kv, halo, extra),
            [SMEM] + [VMEM] * 7,
            [VMEM] * 3,
            [staged_dq, shape((2, heads, WINDOW, size), emit), shape((2, heads, WINDOW, size), BF16)],
            [],
            20,
            cost(half * 2),
        )

    early_dq, first_other, back_other = early(0, halo_other, part_other, shared, by_head(early_chunks), BF16)
    back_other = shift(back_other, "ctx", -1)
    first_other = swap(first_other)
    own_late_dq, part_mine = call(
        functools.partial(late_kernel, chunks=late_chunks, group=group),
        (sel, low, rows, grads, lead, kv, tail),
        [SMEM] + [VMEM] * 6,
        [VMEM] * 2,
        [staged(late_chunks), shape((2, half, tokens, size), F32)],
        [],
        20,
        cost(half * len(late_chunks)),
    )
    own_early_dq, early_mine, back_mine = early(1, halo_mine, lead, half, staged(early_chunks), F32)
    back_mine = shift(back_mine, "ctx", -1)
    last_other = part_other[:, :, WINDOW:]
    last_other = last_other.at[:, :, tokens - 2 * WINDOW :].add(back_other.astype(F32)).astype(BF16)
    last_other = swap(last_other)
    query_grad = call(
        functools.partial(moved_kernel, chunks=late_chunks, group=group),
        (sel, docs, low, rows, grads, kv, tail, halo_mine, own_early_dq, own_late_dq, early_dq, late_dq),
        [SMEM] + [VMEM] * 11,
        ANY,
        shape(rows.shape, BF16),
        [pltpu.VMEM((chunks, CHUNK, half * group, size), BF16), dma((2 * chunks,))],
        20,
        cost(chunks),
    )
    out = shape((tokens, half, size), BF16)
    key_grad, value_grad = call(
        begin_kernel,
        (early_mine, first_other, part_mine),
        [VMEM] * 3,
        [ANY, ANY],
        [out, out],
        [pltpu.VMEM((2, WINDOW, half, size), BF16), dma((2,))],
        8,
    )
    key_grad, value_grad = call(
        finish_kernel,
        (part_mine, last_other, back_mine, key_grad, value_grad),
        [VMEM] * 3 + [ANY] * 2,
        [ANY, ANY],
        [out, out],
        [pltpu.VMEM((2, rest, half, size), BF16), dma((2,))],
        8,
        aliases={3: 0, 4: 1},
    )
    return query_grad.reshape(queries.shape), key_grad, value_grad


def solution(mesh):
    in_specs = (
        P("ctx", None, "head", None),
        P("ctx", None, None),
        P("ctx", None, None),
        P("ctx", None, "head", None),
        P("ctx"),
    )
    out_specs = (P("ctx", None, "head", None), P("ctx", "head", None), P("ctx", "head", None))

    return jax.shard_map(on_device, mesh=mesh, in_specs=in_specs, out_specs=out_specs, check_vma=False)
```

```python
import functools

import jax
import jax.numpy as jnp
from jax import lax
from jax.experimental import pallas as pl
from jax.experimental.pallas import tpu as pltpu
from jax.sharding import PartitionSpec as P


WINDOW = 256
CHUNK = WINDOW // 2
PAD = 8
STEP = 32
MOVED = 1
LOG2E = 1.4426950408889634
F32 = jnp.float32
BF16 = jnp.bfloat16
VMEM = pl.BlockSpec(memory_space=pltpu.VMEM)
SMEM = pl.BlockSpec(memory_space=pltpu.SMEM)
ANY = pl.BlockSpec(memory_space=pl.ANY)
HBM = pl.BlockSpec(memory_space=pltpu.HBM)
MIB = 1024 * 1024


def dot(a, b, contract):
    return lax.dot_general(a, b, (((contract[0],), (contract[1],)), ((), ())), preferred_element_type=F32)


def params(limit):
    return pltpu.CompilerParams(vmem_limit_bytes=limit * MIB)


def count_smaller(column, row):
    return jnp.sum((column < row).astype(F32), axis=0, keepdims=True)


def to_heads(ref, out, i):
    for r in range(0, out.shape[2], STEP):
        out[i, :, r : r + STEP] = jnp.transpose(ref[r : r + STEP], (1, 0, 2))


def tail_kernel(
    sel_ref, key_ref, value_ref, docs_ref, q_ref, do_ref, kv_ref, other_ref, mine_ref, raw_ref, lead_ref, buf, docs_buf, sem
):
    half = key_ref.shape[1] // 2
    chunks = docs_ref.shape[0]
    first = key_ref.shape[0] - WINDOW
    moved = pl.ds(sel_ref[0] * half + half - MOVED, MOVED)
    pairs = [(docs_ref, docs_buf)]
    pairs += [(ref.at[pl.ds(first, WINDOW)], buf.at[i]) for i, ref in enumerate((key_ref, value_ref))]
    pairs += [(ref.at[:, moved], lead_ref.at[i]) for i, ref in enumerate((q_ref, do_ref))]
    pairs += [(ref.at[pl.ds(0, first)], raw_ref.at[i]) for i, ref in enumerate((key_ref, value_ref))]
    copies = [pltpu.make_async_copy(*pair, sem.at[n]) for n, pair in enumerate(pairs)]
    for copy in copies:
        copy.start()
    copies[0].wait()
    pad = jnp.zeros((PAD - 2, CHUNK), BF16)
    tail = jnp.concatenate([docs_buf[chunks - 2 :].astype(F32).astype(BF16), pad], 0)
    for out in (other_ref, mine_ref):
        out[out.shape[0] - PAD :] = tail
    for i in range(2):
        copies[1 + i].wait()
        to_heads(buf.at[i], kv_ref, i)
        for h in range(half):
            out, slot = (other_ref, h) if h < half - MOVED else (mine_ref, h + MOVED)
            out[halo_rows(out, i, slot)] = kv_ref[i, sel_ref[0] * half + h]
            mine_ref[halo_rows(mine_ref, i, h)] = kv_ref[i, sel_ref[1] * half + h]
    for copy in copies[3:]:
        copy.wait()


def interleave(rows, group):
    shape = (rows.shape[1], rows.shape[1] * group)
    source = lax.div(lax.broadcasted_iota(jnp.int32, shape, 1), jnp.int32(group))
    pick = (lax.broadcasted_iota(jnp.int32, shape, 0) == source).astype(F32).astype(BF16)
    return dot(rows.astype(BF16), pick, (1, 0))


def rest_of_block(raw_ref, docs_ref, kv_ref, low_ref, group):
    chunks = docs_ref.shape[0]
    docs = docs_ref[...].astype(F32)
    columns = docs.T
    counts = []
    for c in range(chunks):
        row = docs[c : c + 1]
        counts.append(sum(count_smaller(columns[:, b : b + 1], row) for b in range(c + 1)))
    counts = jnp.concatenate(counts, 0)
    coarse = jnp.floor(counts * (1.0 / CHUNK))
    split = interleave(jnp.concatenate([coarse, counts - coarse * CHUNK], 0), group)
    mixed = split[:chunks] * CHUNK + split[chunks:]
    base = WINDOW - CHUNK * lax.broadcasted_iota(jnp.int32, (chunks, CHUNK * group), 0)
    low_ref[0] = jnp.concatenate([counts] * group, 1).astype(jnp.int32) + base
    low_ref[1] = mixed.astype(jnp.int32) + base
    for i in range(2):
        to_heads(raw_ref.at[i], kv_ref, i)


def half_grads(items, get_query, get_keys, get_low, scale, group, put_dq, put_block):
    cols = CHUNK * group
    row = lax.broadcasted_iota(jnp.int32, (CHUNK, cols), 0)
    col = lax.broadcasted_iota(jnp.int32, (CHUNK, cols), 1)
    middle = row + CHUNK
    masks = {}
    for source in sorted({item[2] for item in items}):
        old = row > (lax.div(col, jnp.int32(group)) if source else col & (CHUNK - 1))
        old_low = old.astype(F32).astype(BF16)
        masks[source] = (old, jnp.where(old, row, row + 2 * CHUNK), old_low, 1 - old_low)
    dqs, sums, state, left = {}, {}, {}, {}
    for c, h, _, _, keys in items:
        for b in range(3 * keys):
            left[h, c + b] = left.get((h, c + b), 0) + 1
    pending = {}
    for c, h, _, query, _ in items:
        pending[c] = pending.get(c, 0) + query

    def scores(item):
        c, h, source, _, _ = item
        q, do = get_query(c, h, source)
        k, v = get_keys(h, c)
        state[item] = (q, do, k, dot(k, q, (1, 1)), dot(v, do, (1, 1)))

    def soft(item):
        q, do, k, s, dp = state[item]
        old, position, old_low, new_low = masks[item[2]]
        low = get_low(item[0], item[2])
        s = [
            jnp.where(position >= low, jnp.where(old, s[:CHUNK], s[2 * CHUNK :]), -1e30),
            jnp.where(middle >= low, s[CHUNK : 2 * CHUNK], -1e30),
        ]
        dp = [jnp.where(old, dp[:CHUNK], dp[2 * CHUNK :]), dp[CHUNK : 2 * CHUNK]]
        top = functools.reduce(jnp.maximum, [jnp.max(x, axis=0, keepdims=True) for x in s])
        w = [jnp.exp2((x - top) * (scale * LOG2E)) for x in s]
        total = sum(jnp.sum(x, axis=0, keepdims=True) for x in w)
        inverse = 1.0 / total
        p = [x * inverse for x in w]
        delta = sum(jnp.sum(x * y, axis=0, keepdims=True) for x, y in zip(p, dp))
        ds = [(x * (y - delta)).astype(BF16) for x, y in zip(p, dp)]
        p = [x.astype(BF16) for x in p]
        p = jnp.concatenate([p[0] * old_low, p[1], p[0] * new_low], 0) if item[4] else None
        ds = jnp.concatenate([ds[0] * old_low, ds[1], ds[0] * new_low], 0)
        state[item] = (q, do, k, p, ds)

    def grads(item):
        c, h, _, query, keys = item
        q, do, k, p, ds = state.pop(item)
        if keys:
            dv = dot(p, do, (1, 0))
            dk = dot(ds, q, (1, 0))
        for b in range(3 * keys):
            rows = slice(b * CHUNK, (b + 1) * CHUNK)
            key = (h, c + b)
            new = (dk[rows], dv[rows])
            if key in sums:
                new = (sums[key][0] + new[0], sums[key][1] + new[1])
            sums[key] = new
            left[key] -= 1
            if not left[key]:
                put_block(h, c + b, *sums.pop(key))
        if query:
            dqs[c, h] = (dot(k.T, ds, (1, 0)) * scale).T.astype(BF16).reshape(group, CHUNK, -1)
            pending[c] -= 1
            if not pending[c]:
                heads = sorted(i for a, i in dqs if a == c)
                put_dq(c, jnp.concatenate([dqs.pop((c, i)) for i in heads], 0))

    scores(items[0])
    for n, item in enumerate(items):
        if n + 1 < len(items):
            scores(items[n + 1])
        if n:
            grads(items[n - 1])
        soft(item)
    grads(items[-1])


def store_before(dq_ref, staged_ref, sem, first, sel, chunks, rows):
    where = pl.ds(pl.multiple_of(sel * rows, rows), rows)
    return [
        pltpu.make_async_copy(
            staged_ref.at[c], dq_ref.at[pl.ds(chunk * CHUNK, CHUNK), where, :], sem.at[first + c]
        )
        for c, chunk in enumerate(chunks)
    ]


def run_half(sel, chunks, items, group, half, q_ref, do_ref, lead_ref, get_keys, get_low, put_block, staged_ref):
    rows = half * group
    size = q_ref.shape[-1]
    where = pl.ds(pl.multiple_of(sel * rows, rows), rows)
    held = {}

    def get_query(c, h, source):
        if source:
            columns = slice(chunks[c] * CHUNK * group, (chunks[c] + 1) * CHUNK * group)
            return lead_ref[0, columns], lead_ref[1, columns]
        if c not in held:
            tokens = slice(chunks[c] * CHUNK, (chunks[c] + 1) * CHUNK)
            held[c] = [jnp.transpose(ref[tokens, where, :], (1, 0, 2)) for ref in (q_ref, do_ref)]
        return [x[h * group : (h + 1) * group].reshape(group * CHUNK, size) for x in held[c]]

    def put_dq(c, value):
        staged_ref[c] = jnp.transpose(value, (1, 0, 2)) if value.shape[0] == rows else value

    half_grads(items, get_query, get_keys, get_low, 1.0 / size**0.5, group, put_dq, put_block)


def partner_items(chunks, half):
    return [(c, h, 0, True, True) for c in range(len(chunks)) for h in range(half - MOVED)]


def own_items(chunks, half):
    items = []
    for c in range(len(chunks)):
        items += [(c, h, 0, True, True) for h in range(half)]
        items += [(c, half - MOVED, 1, False, True)]
    return items


def block_keys(rest_ref, tail_ref, head, chunk):
    rest = rest_ref.shape[2]
    start, stop = (chunk - 2) * CHUNK, (chunk + 1) * CHUNK
    pieces = []
    for i in range(2):
        parts = []
        if start < rest:
            parts.append(rest_ref[i, head, start : min(stop, rest)])
        if stop > rest:
            parts.append(tail_ref[i, head, max(start - rest, 0) : stop - rest])
        pieces.append(jnp.concatenate(parts, 0))
    return pieces


def halo_rows(ref, i, slot):
    heads = (ref.shape[0] - PAD) // (2 * WINDOW)
    return slice((i * heads + slot) * WINDOW, (i * heads + slot + 1) * WINDOW)


def halo_keys(halo_ref, rest_ref, slot, head, chunk):
    return [
        jnp.concatenate([halo_ref[halo_rows(halo_ref, i, slot)][chunk * CHUNK :], rest_ref[i, head, : (chunk + 1) * CHUNK]], 0)
        for i in range(2)
    ]


def early_lows(sel_ref, docs_ref, low_ref, halo_ref, group, mixed):
    ahead = jnp.where(sel_ref[2] == 0, -1.0, halo_ref[halo_ref.shape[0] - PAD :].astype(F32)).T
    counts = []
    for c in range(2):
        docs = docs_ref[c : c + 1, :].astype(F32)
        counts += [count_smaller(ahead[:, b : b + 1], docs) for b in range(2)]
    lows = {}
    if mixed:
        spread = interleave(jnp.concatenate(counts, 0), group)
    for c in range(2):
        count = jnp.concatenate([counts[2 * c] + counts[2 * c + 1]] * group, 1)
        lows[c, 0] = low_ref[0, c : c + 1, :] - WINDOW + count.astype(jnp.int32)
        if mixed:
            count = spread[2 * c : 2 * c + 1] + spread[2 * c + 1 : 2 * c + 2]
            lows[c, 1] = low_ref[1, c : c + 1, :] - WINDOW + count.astype(jnp.int32)
    return lows


def run_late(sel, chunks, items, group, half, q_ref, do_ref, lead_ref, rest_ref, tail_ref, low_ref, staged_ref, part_ref):
    scale = 1.0 / part_ref.shape[-1] ** 0.5

    def get_keys(h, c):
        return block_keys(rest_ref, tail_ref, sel * half + h, chunks[c])

    def put_block(h, b, dk, dv):
        block = slice((chunks[0] - 2 + b) * CHUNK, (chunks[0] - 1 + b) * CHUNK)
        part_ref[0, h, block] = dk * scale
        part_ref[1, h, block] = dv

    def get_low(c, source):
        return low_ref[source, chunks[c] : chunks[c] + 1, :]

    run_half(sel, chunks, items, group, half, q_ref, do_ref, lead_ref, get_keys, get_low, put_block, staged_ref)


def first_kernel(
    sel_ref, docs_ref, raw_ref, tail_ref, q_ref, do_ref, staged_ref, part_ref, kv_ref, low_ref, *, chunks, group
):
    half = kv_ref.shape[1] // 2
    rest_of_block(raw_ref, docs_ref, kv_ref, low_ref, group)
    items = partner_items(chunks, half)
    run_late(
        sel_ref[0], chunks, items, group, half, q_ref, do_ref, None, kv_ref, tail_ref, low_ref, staged_ref, part_ref
    )


def late_kernel(
    sel_ref, low_ref, q_ref, do_ref, lead_ref, rest_ref, tail_ref, staged_ref, part_ref, *, chunks, group
):
    half = part_ref.shape[1]
    items = own_items(chunks, half)
    run_late(
        sel_ref[1], chunks, items, group, half, q_ref, do_ref, lead_ref, rest_ref, tail_ref, low_ref, staged_ref, part_ref
    )


def moved_kernel(
    sel_ref, docs_ref, low_ref, q_ref, do_ref, rest_ref, tail_ref, halo_ref, own_early_ref, own_late_ref, early_ref, late_ref,
    dq_ref, buf, sem, *, chunks, group
):
    half = rest_ref.shape[1] // 2
    rows = half * group
    size = q_ref.shape[-1]
    early = own_early_ref.shape[0]
    total = early + len(chunks)
    copies = store_before(dq_ref, own_early_ref, sem, 0, sel_ref[1], range(early), rows)
    copies += store_before(dq_ref, own_late_ref, sem, early, sel_ref[1], chunks, rows)
    for copy in copies:
        copy.start()
    where = pl.ds(pl.multiple_of(sel_ref[0] * rows, rows), rows)
    head = sel_ref[0] * half + half - MOVED
    lows = early_lows(sel_ref, docs_ref, low_ref, halo_ref, group, False)

    def store(c):
        target = dq_ref.at[pl.ds(c * CHUNK, CHUNK), where, :]
        return pltpu.make_async_copy(buf.at[c], target, sem.at[total + c])

    def get_query(c, h, source):
        tokens = slice(c * CHUNK, (c + 1) * CHUNK)
        both = [jnp.transpose(ref[tokens, where, :], (1, 0, 2)) for ref in (q_ref, do_ref)]
        return [x[rows - MOVED * group :].reshape(group * CHUNK, size) for x in both]

    def get_keys(h, c):
        return halo_keys(halo_ref, rest_ref, half, head, c) if c < early else block_keys(rest_ref, tail_ref, head, c)

    def get_low(c, source):
        return lows[c, 0] if c < early else low_ref[0, c : c + 1, :]

    def put_dq(c, value):
        others = early_ref[c] if c < early else late_ref[c - early]
        buf[c] = jnp.transpose(jnp.concatenate([others, value], 0), (1, 0, 2))
        store(c).start()

    items = [(c, 0, 0, True, False) for c in range(total)]
    half_grads(items, get_query, get_keys, get_low, 1.0 / size**0.5, group, put_dq, None)
    for copy in copies:
        copy.wait()
    for c in range(total):
        store(c).wait()


def early_kernel(
    sel_ref, docs_ref, low_ref, q_ref, do_ref, rest_ref, halo_ref, extra_ref, staged_ref, own_ref, back_ref, *, group, n
):
    half = rest_ref.shape[1] // 2
    scale = 1.0 / own_ref.shape[-1] ** 0.5
    sel = sel_ref[n]
    lows = early_lows(sel_ref, docs_ref, low_ref, halo_ref, group, n > 0)

    def get_keys(h, c):
        return halo_keys(halo_ref, rest_ref, h, sel * half + h, c)

    def put_block(h, b, dk, dv):
        dk = dk * scale
        if b < 2:
            block = slice(b * CHUNK, (b + 1) * CHUNK)
            back_ref[0, h, block] = dk.astype(BF16)
            back_ref[1, h, block] = dv.astype(BF16)
        else:
            block = slice((b - 2) * CHUNK, (b - 1) * CHUNK)
            if not n:
                dk, dv = dk + extra_ref[0, h, block], dv + extra_ref[1, h, block]
            own_ref[0, h, block] = dk.astype(own_ref.dtype)
            own_ref[1, h, block] = dv.astype(own_ref.dtype)

    items = own_items((0, 1), half) if n else partner_items((0, 1), half)
    run_half(
        sel, (0, 1), items, group, half, q_ref, do_ref, extra_ref if n else None, get_keys,
        lambda c, source: lows[c, source], put_block, staged_ref
    )


def out_rows(buf, sem, i, out, rows):
    return pltpu.make_async_copy(buf.at[i], out.at[rows], sem.at[i])


def begin_kernel(early_ref, first_in, part_ref, dk_ref, dv_ref, buf, sem):
    shared = first_in.shape[1]
    for i, out in ((0, dk_ref), (1, dv_ref)):
        for r in range(0, WINDOW, STEP):
            rows = slice(r, r + STEP)
            value = early_ref[i, :, rows] + part_ref[i, :, rows]
            value = jnp.concatenate([value[:shared] + first_in[i, :, rows].astype(F32), value[shared:]], 0)
            buf[i, rows] = jnp.transpose(value.astype(BF16), (1, 0, 2))
        out_rows(buf, sem, i, out, pl.ds(0, WINDOW)).start()
    for i, out in ((0, dk_ref), (1, dv_ref)):
        out_rows(buf, sem, i, out, pl.ds(0, WINDOW)).wait()


def finish_kernel(part_ref, last_in, back_in, dk_in, dv_in, dk_ref, dv_ref, buf, sem):
    late = part_ref.shape[2] - WINDOW
    shared = last_in.shape[1]
    for i, out in ((0, dk_ref), (1, dv_ref)):
        for r in range(0, late, STEP):
            rows = slice(r, r + STEP)
            value = part_ref[i, :, WINDOW + r : WINDOW + r + STEP]
            skip = late - WINDOW
            if r >= skip:
                value = value + back_in[i, :, r - skip : r - skip + STEP].astype(F32)
            value = jnp.concatenate([value[:shared] + last_in[i, :, rows].astype(F32), value[shared:]], 0)
            buf[i, rows] = jnp.transpose(value.astype(BF16), (1, 0, 2))
        out_rows(buf, sem, i, out, pl.ds(WINDOW, late)).start()
    for i, out in ((0, dk_ref), (1, dv_ref)):
        out_rows(buf, sem, i, out, pl.ds(WINDOW, late)).wait()


def shift(block, axis, distance):
    devices = range(lax.axis_size(axis))
    return lax.ppermute(block, axis, [(i - distance, i) for i in devices if i - distance in devices])


def swap(block):
    return lax.ppermute(block, "head", [(0, 1), (1, 0)])


def in_hbm(array):
    return pltpu.with_memory_space_constraint(array, pltpu.HBM)


def on_device(queries, key_heads, value_heads, out_grad, doc_ids):
    tokens, kv_count, group, size = queries.shape
    half = kv_count // 2
    shared = half - MOVED
    chunks = tokens // CHUNK
    rest = tokens - WINDOW
    shape = jax.ShapeDtypeStruct
    dma = pltpu.SemaphoreType.DMA
    head = lax.axis_index("head")
    sel = jnp.stack([1 - head, head, lax.axis_index("ctx")]).astype(jnp.int32)
    rows = queries.reshape(tokens, kv_count * group, size)
    grads = out_grad.reshape(tokens, kv_count * group, size)
    docs = doc_ids.reshape(chunks, CHUNK)

    def halo_shape(heads):
        return shape((2 * heads * WINDOW + PAD, size), BF16)

    early_chunks, late_chunks = (0, 1), tuple(range(2, chunks))

    def cost(n):
        work = n * 10 * CHUNK * group * (WINDOW + CHUNK) * size
        return pl.CostEstimate(flops=work * 10, bytes_accessed=n * CHUNK * group * size * 8, transcendentals=0)

    def staged(chunks):
        return shape((len(chunks), CHUNK, half * group, size), BF16)

    def by_head(chunks):
        return shape((len(chunks), shared * group, CHUNK, size), BF16)

    def call(body, operands, specs, out_specs, out_shape, scratch, limit, estimate=None, aliases=None):
        return pl.pallas_call(
            body,
            in_specs=specs,
            out_specs=out_specs,
            out_shape=out_shape,
            scratch_shapes=scratch,
            input_output_aliases=aliases or {},
            compiler_params=params(limit),
            cost_estimate=estimate,
        )(*operands)

    tail, halo_other, halo_mine, raw, lead = call(
        tail_kernel,
        (sel, in_hbm(key_heads), in_hbm(value_heads), in_hbm(docs), in_hbm(queries), in_hbm(out_grad)),
        [SMEM] + [HBM] * 5,
        [VMEM] * 5,
        [
            shape((2, kv_count, WINDOW, size), BF16),
            halo_shape(shared),
            halo_shape(half + MOVED),
            shape((2, rest, kv_count, size), BF16),
            shape((2, tokens, MOVED, group, size), BF16),
        ],
        [pltpu.VMEM((2, WINDOW, kv_count, size), BF16), pltpu.VMEM(docs.shape, docs.dtype), dma((7,))],
        16,
    )
    halo_other = shift(halo_other, "ctx", 1)
    halo_mine = shift(halo_mine, "ctx", 1)
    lead = swap(lead).reshape(2, tokens * group, size)
    late_dq, part_other, kv, low = call(
        functools.partial(first_kernel, chunks=late_chunks, group=group),
        (sel, docs, raw, tail, rows, grads),
        [SMEM] + [VMEM] * 5,
        [VMEM] * 4,
        [
            by_head(late_chunks),
            shape((2, shared, tokens, size), F32),
            shape((2, kv_count, rest, size), BF16),
            shape((2, chunks, CHUNK * group), jnp.int32),
        ],
        [],
        20,
        cost(half * len(late_chunks)),
    )

    def early(n, halo, extra, heads, staged_dq, emit):
        return call(
            functools.partial(early_kernel, group=group, n=n),
            (sel, docs, low, rows, grads, kv, halo, extra),
            [SMEM] + [VMEM] * 7,
            [VMEM] * 3,
            [staged_dq, shape((2, heads, WINDOW, size), emit), shape((2, heads, WINDOW, size), BF16)],
            [],
            20,
            cost(half * 2),
        )

    early_dq, first_other, back_other = early(0, halo_other, part_other, shared, by_head(early_chunks), BF16)
    back_other = shift(back_other, "ctx", -1)
    first_other = swap(first_other)
    own_late_dq, part_mine = call(
        functools.partial(late_kernel, chunks=late_chunks, group=group),
        (sel, low, rows, grads, lead, kv, tail),
        [SMEM] + [VMEM] * 6,
        [VMEM] * 2,
        [staged(late_chunks), shape((2, half, tokens, size), F32)],
        [],
        20,
        cost(half * len(late_chunks)),
    )
    own_early_dq, early_mine, back_mine = early(1, halo_mine, lead, half, staged(early_chunks), F32)
    back_mine = shift(back_mine, "ctx", -1)
    last_other = part_other[:, :, WINDOW:]
    last_other = last_other.at[:, :, tokens - 2 * WINDOW :].add(back_other.astype(F32)).astype(BF16)
    last_other = swap(last_other)
    query_grad = call(
        functools.partial(moved_kernel, chunks=late_chunks, group=group),
        (sel, docs, low, rows, grads, kv, tail, halo_mine, own_early_dq, own_late_dq, early_dq, late_dq),
        [SMEM] + [VMEM] * 11,
        ANY,
        shape(rows.shape, BF16),
        [pltpu.VMEM((chunks, CHUNK, half * group, size), BF16), dma((2 * chunks,))],
        20,
        cost(chunks),
    )
    out = shape((tokens, half, size), BF16)
    key_grad, value_grad = call(
        begin_kernel,
        (early_mine, first_other, part_mine),
        [VMEM] * 3,
        [ANY, ANY],
        [out, out],
        [pltpu.VMEM((2, WINDOW, half, size), BF16), dma((2,))],
        8,
    )
    key_grad, value_grad = call(
        finish_kernel,
        (part_mine, last_other, back_mine, key_grad, value_grad),
        [VMEM] * 3 + [ANY] * 2,
        [ANY, ANY],
        [out, out],
        [pltpu.VMEM((2, rest, half, size), BF16), dma((2,))],
        8,
        aliases={3: 0, 4: 1},
    )
    return query_grad.reshape(queries.shape), key_grad, value_grad


def solution(mesh):
    in_specs = (
        P("ctx", None, "head", None),
        P("ctx", None, None),
        P("ctx", None, None),
        P("ctx", None, "head", None),
        P("ctx"),
    )
    out_specs = (P("ctx", None, "head", None), P("ctx", "head", None), P("ctx", "head", None))

    return jax.shard_map(on_device, mesh=mesh, in_specs=in_specs, out_specs=out_specs, check_vma=False)
```

```python
import functools

import jax
import jax.numpy as jnp
from jax import lax
from jax.experimental import pallas as pl
from jax.experimental.pallas import tpu as pltpu
from jax.sharding import PartitionSpec as P


WINDOW = 256
CHUNK = WINDOW // 2
PAD = 8
STEP = 32
MOVED = 1
LOG2E = 1.4426950408889634
F32 = jnp.float32
BF16 = jnp.bfloat16
VMEM = pl.BlockSpec(memory_space=pltpu.VMEM)
SMEM = pl.BlockSpec(memory_space=pltpu.SMEM)
ANY = pl.BlockSpec(memory_space=pl.ANY)
HBM = pl.BlockSpec(memory_space=pltpu.HBM)
MIB = 1024 * 1024


def dot(a, b, contract):
    return lax.dot_general(a, b, (((contract[0],), (contract[1],)), ((), ())), preferred_element_type=F32)


def params(limit):
    return pltpu.CompilerParams(vmem_limit_bytes=limit * MIB)


def count_smaller(column, row):
    return jnp.sum((column < row).astype(F32), axis=0, keepdims=True)


def to_heads(ref, out, i):
    for r in range(0, out.shape[2], STEP):
        out[i, :, r : r + STEP] = jnp.transpose(ref[r : r + STEP], (1, 0, 2))


def tail_kernel(
    sel_ref, key_ref, value_ref, docs_ref, q_ref, do_ref, kv_ref, other_ref, mine_ref, raw_ref, lead_ref, buf, docs_buf, sem
):
    half = key_ref.shape[1] // 2
    chunks = docs_ref.shape[0]
    first = key_ref.shape[0] - WINDOW
    moved = pl.ds(sel_ref[0] * half + half - MOVED, MOVED)
    pairs = [(docs_ref, docs_buf)]
    pairs += [(ref.at[pl.ds(first, WINDOW)], buf.at[i]) for i, ref in enumerate((key_ref, value_ref))]
    pairs += [(ref.at[:, moved], lead_ref.at[i]) for i, ref in enumerate((q_ref, do_ref))]
    pairs += [(ref.at[pl.ds(0, first)], raw_ref.at[i]) for i, ref in enumerate((key_ref, value_ref))]
    copies = [pltpu.make_async_copy(*pair, sem.at[n]) for n, pair in enumerate(pairs)]
    for copy in copies:
        copy.start()
    copies[0].wait()
    pad = jnp.zeros((PAD - 2, CHUNK), BF16)
    tail = jnp.concatenate([docs_buf[chunks - 2 :].astype(F32).astype(BF16), pad], 0)
    for out in (other_ref, mine_ref):
        out[out.shape[0] - PAD :] = tail
    for i in range(2):
        copies[1 + i].wait()
        to_heads(buf.at[i], kv_ref, i)
        for h in range(half):
            out, slot = (other_ref, h) if h < half - MOVED else (mine_ref, h + MOVED)
            out[halo_rows(out, i, slot)] = kv_ref[i, sel_ref[0] * half + h]
            mine_ref[halo_rows(mine_ref, i, h)] = kv_ref[i, sel_ref[1] * half + h]
    for copy in copies[3:]:
        copy.wait()


def interleave(rows, group):
    shape = (rows.shape[1], rows.shape[1] * group)
    source = lax.div(lax.broadcasted_iota(jnp.int32, shape, 1), jnp.int32(group))
    pick = (lax.broadcasted_iota(jnp.int32, shape, 0) == source).astype(F32).astype(BF16)
    return dot(rows.astype(BF16), pick, (1, 0))


def rest_of_block(raw_ref, docs_ref, kv_ref, low_ref, group):
    chunks = docs_ref.shape[0]
    docs = docs_ref[...].astype(F32)
    columns = docs.T
    counts = []
    for c in range(chunks):
        row = docs[c : c + 1]
        counts.append(sum(count_smaller(columns[:, b : b + 1], row) for b in range(c + 1)))
    counts = jnp.concatenate(counts, 0)
    coarse = jnp.floor(counts * (1.0 / CHUNK))
    split = interleave(jnp.concatenate([coarse, counts - coarse * CHUNK], 0), group)
    mixed = split[:chunks] * CHUNK + split[chunks:]
    base = WINDOW - CHUNK * lax.broadcasted_iota(jnp.int32, (chunks, CHUNK * group), 0)
    low_ref[0] = jnp.concatenate([counts] * group, 1).astype(jnp.int32) + base
    low_ref[1] = mixed.astype(jnp.int32) + base
    for i in range(2):
        to_heads(raw_ref.at[i], kv_ref, i)


def half_grads(items, get_query, get_keys, get_low, scale, group, put_dq, put_block):
    cols = CHUNK * group
    row = lax.broadcasted_iota(jnp.int32, (CHUNK, cols), 0)
    col = lax.broadcasted_iota(jnp.int32, (CHUNK, cols), 1)
    middle = row + CHUNK
    masks = {}
    for source in sorted({item[2] for item in items}):
        old = row > (lax.div(col, jnp.int32(group)) if source else col & (CHUNK - 1))
        old_low = old.astype(F32).astype(BF16)
        masks[source] = (old, jnp.where(old, row, row + 2 * CHUNK), old_low, 1 - old_low)
    dqs, sums, state, left = {}, {}, {}, {}
    for c, h, _, _, keys in items:
        for b in range(3 * keys):
            left[h, c + b] = left.get((h, c + b), 0) + 1
    pending = {}
    for c, h, _, query, _ in items:
        pending[c] = pending.get(c, 0) + query

    def scores(item):
        c, h, source, _, _ = item
        q, do = get_query(c, h, source)
        k, v = get_keys(h, c)
        state[item] = (q, do, k, dot(k, q, (1, 1)), dot(v, do, (1, 1)))

    def soft(item):
        q, do, k, s, dp = state[item]
        old, position, old_low, new_low = masks[item[2]]
        low = get_low(item[0], item[2])
        s = [
            jnp.where(position >= low, jnp.where(old, s[:CHUNK], s[2 * CHUNK :]), -1e30),
            jnp.where(middle >= low, s[CHUNK : 2 * CHUNK], -1e30),
        ]
        dp = [jnp.where(old, dp[:CHUNK], dp[2 * CHUNK :]), dp[CHUNK : 2 * CHUNK]]
        top = functools.reduce(jnp.maximum, [jnp.max(x, axis=0, keepdims=True) for x in s])
        w = [jnp.exp2((x - top) * (scale * LOG2E)) for x in s]
        total = sum(jnp.sum(x, axis=0, keepdims=True) for x in w)
        inverse = 1.0 / total
        p = [x * inverse for x in w]
        delta = sum(jnp.sum(x * y, axis=0, keepdims=True) for x, y in zip(p, dp))
        ds = [(x * (y - delta)).astype(BF16) for x, y in zip(p, dp)]
        p = [x.astype(BF16) for x in p]
        p = jnp.concatenate([p[0] * old_low, p[1], p[0] * new_low], 0) if item[4] else None
        ds = jnp.concatenate([ds[0] * old_low, ds[1], ds[0] * new_low], 0)
        state[item] = (q, do, k, p, ds)

    def grads(item):
        c, h, _, query, keys = item
        q, do, k, p, ds = state.pop(item)
        if keys:
            dv = dot(p, do, (1, 0))
            dk = dot(ds, q, (1, 0))
        for b in range(3 * keys):
            rows = slice(b * CHUNK, (b + 1) * CHUNK)
            key = (h, c + b)
            new = (dk[rows], dv[rows])
            if key in sums:
                new = (sums[key][0] + new[0], sums[key][1] + new[1])
            sums[key] = new
            left[key] -= 1
            if not left[key]:
                put_block(h, c + b, *sums.pop(key))
        if query:
            dqs[c, h] = (dot(k.T, ds, (1, 0)) * scale).T.astype(BF16).reshape(group, CHUNK, -1)
            pending[c] -= 1
            if not pending[c]:
                heads = sorted(i for a, i in dqs if a == c)
                put_dq(c, jnp.concatenate([dqs.pop((c, i)) for i in heads], 0))

    scores(items[0])
    for n, item in enumerate(items):
        if n + 1 < len(items):
            scores(items[n + 1])
        if n:
            grads(items[n - 1])
        soft(item)
    grads(items[-1])


def store_before(dq_ref, staged_ref, sem, first, sel, chunks, rows):
    where = pl.ds(pl.multiple_of(sel * rows, rows), rows)
    return [
        pltpu.make_async_copy(
            staged_ref.at[c], dq_ref.at[pl.ds(chunk * CHUNK, CHUNK), where, :], sem.at[first + c]
        )
        for c, chunk in enumerate(chunks)
    ]


def run_half(sel, chunks, items, group, half, q_ref, do_ref, lead_ref, get_keys, get_low, put_block, staged_ref):
    rows = half * group
    size = q_ref.shape[-1]
    where = pl.ds(pl.multiple_of(sel * rows, rows), rows)
    held = {}

    def get_query(c, h, source):
        if source:
            columns = slice(chunks[c] * CHUNK * group, (chunks[c] + 1) * CHUNK * group)
            return lead_ref[0, columns], lead_ref[1, columns]
        if c not in held:
            tokens = slice(chunks[c] * CHUNK, (chunks[c] + 1) * CHUNK)
            held[c] = [jnp.transpose(ref[tokens, where, :], (1, 0, 2)) for ref in (q_ref, do_ref)]
        return [x[h * group : (h + 1) * group].reshape(group * CHUNK, size) for x in held[c]]

    def put_dq(c, value):
        staged_ref[c] = jnp.transpose(value, (1, 0, 2)) if value.shape[0] == rows else value

    half_grads(items, get_query, get_keys, get_low, 1.0 / size**0.5, group, put_dq, put_block)


def partner_items(chunks, half):
    return [(c, h, 0, True, True) for c in range(len(chunks)) for h in range(half - MOVED)]


def own_items(chunks, half):
    items = []
    for c in range(len(chunks)):
        items += [(c, h, 0, True, True) for h in range(half)]
        items += [(c, half - MOVED, 1, False, True)]
    return items


def block_keys(rest_ref, tail_ref, head, chunk):
    rest = rest_ref.shape[2]
    start, stop = (chunk - 2) * CHUNK, (chunk + 1) * CHUNK
    pieces = []
    for i in range(2):
        parts = []
        if start < rest:
            parts.append(rest_ref[i, head, start : min(stop, rest)])
        if stop > rest:
            parts.append(tail_ref[i, head, max(start - rest, 0) : stop - rest])
        pieces.append(jnp.concatenate(parts, 0))
    return pieces


def halo_rows(ref, i, slot):
    heads = (ref.shape[0] - PAD) // (2 * WINDOW)
    return slice((i * heads + slot) * WINDOW, (i * heads + slot + 1) * WINDOW)


def halo_keys(halo_ref, rest_ref, slot, head, chunk):
    return [
        jnp.concatenate([halo_ref[halo_rows(halo_ref, i, slot)][chunk * CHUNK :], rest_ref[i, head, : (chunk + 1) * CHUNK]], 0)
        for i in range(2)
    ]


def early_lows(sel_ref, docs_ref, low_ref, halo_ref, group, mixed):
    ahead = jnp.where(sel_ref[2] == 0, -1.0, halo_ref[halo_ref.shape[0] - PAD :].astype(F32)).T
    counts = []
    for c in range(2):
        docs = docs_ref[c : c + 1, :].astype(F32)
        counts += [count_smaller(ahead[:, b : b + 1], docs) for b in range(2)]
    lows = {}
    if mixed:
        spread = interleave(jnp.concatenate(counts, 0), group)
    for c in range(2):
        count = jnp.concatenate([counts[2 * c] + counts[2 * c + 1]] * group, 1)
        lows[c, 0] = low_ref[0, c : c + 1, :] - WINDOW + count.astype(jnp.int32)
        if mixed:
            count = spread[2 * c : 2 * c + 1] + spread[2 * c + 1 : 2 * c + 2]
            lows[c, 1] = low_ref[1, c : c + 1, :] - WINDOW + count.astype(jnp.int32)
    return lows


def run_late(sel, chunks, items, group, half, q_ref, do_ref, lead_ref, rest_ref, tail_ref, low_ref, staged_ref, part_ref):
    scale = 1.0 / part_ref.shape[-1] ** 0.5

    def get_keys(h, c):
        return block_keys(rest_ref, tail_ref, sel * half + h, chunks[c])

    def put_block(h, b, dk, dv):
        block = slice((chunks[0] - 2 + b) * CHUNK, (chunks[0] - 1 + b) * CHUNK)
        part_ref[0, h, block] = dk * scale
        part_ref[1, h, block] = dv

    def get_low(c, source):
        return low_ref[source, chunks[c] : chunks[c] + 1, :]

    run_half(sel, chunks, items, group, half, q_ref, do_ref, lead_ref, get_keys, get_low, put_block, staged_ref)


def first_kernel(
    sel_ref, docs_ref, raw_ref, tail_ref, q_ref, do_ref, staged_ref, part_ref, kv_ref, low_ref, *, chunks, group
):
    half = kv_ref.shape[1] // 2
    rest_of_block(raw_ref, docs_ref, kv_ref, low_ref, group)
    items = partner_items(chunks, half)
    run_late(
        sel_ref[0], chunks, items, group, half, q_ref, do_ref, None, kv_ref, tail_ref, low_ref, staged_ref, part_ref
    )


def late_kernel(
    sel_ref, low_ref, q_ref, do_ref, lead_ref, rest_ref, tail_ref, staged_ref, part_ref, *, chunks, group
):
    half = part_ref.shape[1]
    items = own_items(chunks, half)
    run_late(
        sel_ref[1], chunks, items, group, half, q_ref, do_ref, lead_ref, rest_ref, tail_ref, low_ref, staged_ref, part_ref
    )


def moved_kernel(
    sel_ref, docs_ref, low_ref, q_ref, do_ref, rest_ref, tail_ref, halo_ref, own_early_ref, own_late_ref, early_ref, late_ref,
    dq_ref, buf, sem, *, chunks, group
):
    half = rest_ref.shape[1] // 2
    rows = half * group
    size = q_ref.shape[-1]
    early = own_early_ref.shape[0]
    total = early + len(chunks)
    copies = store_before(dq_ref, own_early_ref, sem, 0, sel_ref[1], range(early), rows)
    copies += store_before(dq_ref, own_late_ref, sem, early, sel_ref[1], chunks, rows)
    for copy in copies:
        copy.start()
    where = pl.ds(pl.multiple_of(sel_ref[0] * rows, rows), rows)
    head = sel_ref[0] * half + half - MOVED
    lows = early_lows(sel_ref, docs_ref, low_ref, halo_ref, group, False)

    def store(c):
        target = dq_ref.at[pl.ds(c * CHUNK, CHUNK), where, :]
        return pltpu.make_async_copy(buf.at[c], target, sem.at[total + c])

    def get_query(c, h, source):
        tokens = slice(c * CHUNK, (c + 1) * CHUNK)
        both = [jnp.transpose(ref[tokens, where, :], (1, 0, 2)) for ref in (q_ref, do_ref)]
        return [x[rows - MOVED * group :].reshape(group * CHUNK, size) for x in both]

    def get_keys(h, c):
        return halo_keys(halo_ref, rest_ref, half, head, c) if c < early else block_keys(rest_ref, tail_ref, head, c)

    def get_low(c, source):
        return lows[c, 0] if c < early else low_ref[0, c : c + 1, :]

    def put_dq(c, value):
        others = early_ref[c] if c < early else late_ref[c - early]
        buf[c] = jnp.transpose(jnp.concatenate([others, value], 0), (1, 0, 2))
        store(c).start()

    items = [(c, 0, 0, True, False) for c in range(total)]
    half_grads(items, get_query, get_keys, get_low, 1.0 / size**0.5, group, put_dq, None)
    for copy in copies:
        copy.wait()
    for c in range(total):
        store(c).wait()


def early_kernel(
    sel_ref, docs_ref, low_ref, q_ref, do_ref, rest_ref, halo_ref, extra_ref, staged_ref, own_ref, back_ref, *, group, n
):
    half = rest_ref.shape[1] // 2
    scale = 1.0 / own_ref.shape[-1] ** 0.5
    sel = sel_ref[n]
    lows = early_lows(sel_ref, docs_ref, low_ref, halo_ref, group, n > 0)

    def get_keys(h, c):
        return halo_keys(halo_ref, rest_ref, h, sel * half + h, c)

    def put_block(h, b, dk, dv):
        dk = dk * scale
        if b < 2:
            block = slice(b * CHUNK, (b + 1) * CHUNK)
            back_ref[0, h, block] = dk.astype(BF16)
            back_ref[1, h, block] = dv.astype(BF16)
        else:
            block = slice((b - 2) * CHUNK, (b - 1) * CHUNK)
            if not n:
                dk, dv = dk + extra_ref[0, h, block], dv + extra_ref[1, h, block]
            own_ref[0, h, block] = dk.astype(own_ref.dtype)
            own_ref[1, h, block] = dv.astype(own_ref.dtype)

    items = own_items((0, 1), half) if n else partner_items((0, 1), half)
    run_half(
        sel, (0, 1), items, group, half, q_ref, do_ref, extra_ref if n else None, get_keys,
        lambda c, source: lows[c, source], put_block, staged_ref
    )


def out_rows(buf, sem, i, out, rows):
    return pltpu.make_async_copy(buf.at[i], out.at[rows], sem.at[i])


def begin_kernel(early_ref, first_in, part_ref, dk_ref, dv_ref, buf, sem):
    shared = first_in.shape[1]
    for i, out in ((0, dk_ref), (1, dv_ref)):
        for r in range(0, WINDOW, STEP):
            rows = slice(r, r + STEP)
            value = early_ref[i, :, rows] + part_ref[i, :, rows]
            value = jnp.concatenate([value[:shared] + first_in[i, :, rows].astype(F32), value[shared:]], 0)
            buf[i, rows] = jnp.transpose(value.astype(BF16), (1, 0, 2))
        out_rows(buf, sem, i, out, pl.ds(0, WINDOW)).start()
    for i, out in ((0, dk_ref), (1, dv_ref)):
        out_rows(buf, sem, i, out, pl.ds(0, WINDOW)).wait()


def finish_kernel(part_ref, last_in, back_in, dk_in, dv_in, dk_ref, dv_ref, buf, sem):
    late = part_ref.shape[2] - WINDOW
    shared = last_in.shape[1]

    def piece(i, out, n):
        rows = pl.ds(n * CHUNK, CHUNK)
        return pltpu.make_async_copy(buf.at[i, rows], out.at[pl.ds(WINDOW + n * CHUNK, CHUNK)], sem.at[i, n])

    for i, out in ((0, dk_ref), (1, dv_ref)):
        for r in range(0, late, STEP):
            rows = slice(r, r + STEP)
            value = part_ref[i, :, WINDOW + r : WINDOW + r + STEP]
            skip = late - WINDOW
            if r >= skip:
                value = value + back_in[i, :, r - skip : r - skip + STEP].astype(F32)
            value = jnp.concatenate([value[:shared] + last_in[i, :, rows].astype(F32), value[shared:]], 0)
            buf[i, rows] = jnp.transpose(value.astype(BF16), (1, 0, 2))
            if (r + STEP) % CHUNK == 0:
                piece(i, out, r // CHUNK).start()
    for i, out in ((0, dk_ref), (1, dv_ref)):
        for n in range(late // CHUNK):
            piece(i, out, n).wait()


def shift(block, axis, distance):
    devices = range(lax.axis_size(axis))
    return lax.ppermute(block, axis, [(i - distance, i) for i in devices if i - distance in devices])


def swap(block):
    return lax.ppermute(block, "head", [(0, 1), (1, 0)])


def in_hbm(array):
    return pltpu.with_memory_space_constraint(array, pltpu.HBM)


def on_device(queries, key_heads, value_heads, out_grad, doc_ids):
    tokens, kv_count, group, size = queries.shape
    half = kv_count // 2
    shared = half - MOVED
    chunks = tokens // CHUNK
    rest = tokens - WINDOW
    shape = jax.ShapeDtypeStruct
    dma = pltpu.SemaphoreType.DMA
    head = lax.axis_index("head")
    sel = jnp.stack([1 - head, head, lax.axis_index("ctx")]).astype(jnp.int32)
    rows = queries.reshape(tokens, kv_count * group, size)
    grads = out_grad.reshape(tokens, kv_count * group, size)
    docs = doc_ids.reshape(chunks, CHUNK)

    def halo_shape(heads):
        return shape((2 * heads * WINDOW + PAD, size), BF16)

    early_chunks, late_chunks = (0, 1), tuple(range(2, chunks))

    def cost(n):
        work = n * 10 * CHUNK * group * (WINDOW + CHUNK) * size
        return pl.CostEstimate(flops=work * 10, bytes_accessed=n * CHUNK * group * size * 8, transcendentals=0)

    def staged(chunks):
        return shape((len(chunks), CHUNK, half * group, size), BF16)

    def by_head(chunks):
        return shape((len(chunks), shared * group, CHUNK, size), BF16)

    def call(body, operands, specs, out_specs, out_shape, scratch, limit, estimate=None, aliases=None):
        return pl.pallas_call(
            body,
            in_specs=specs,
            out_specs=out_specs,
            out_shape=out_shape,
            scratch_shapes=scratch,
            input_output_aliases=aliases or {},
            compiler_params=params(limit),
            cost_estimate=estimate,
        )(*operands)

    tail, halo_other, halo_mine, raw, lead = call(
        tail_kernel,
        (sel, in_hbm(key_heads), in_hbm(value_heads), in_hbm(docs), in_hbm(queries), in_hbm(out_grad)),
        [SMEM] + [HBM] * 5,
        [VMEM] * 5,
        [
            shape((2, kv_count, WINDOW, size), BF16),
            halo_shape(shared),
            halo_shape(half + MOVED),
            shape((2, rest, kv_count, size), BF16),
            shape((2, tokens, MOVED, group, size), BF16),
        ],
        [pltpu.VMEM((2, WINDOW, kv_count, size), BF16), pltpu.VMEM(docs.shape, docs.dtype), dma((7,))],
        16,
    )
    halo_other = shift(halo_other, "ctx", 1)
    halo_mine = shift(halo_mine, "ctx", 1)
    lead = swap(lead).reshape(2, tokens * group, size)
    late_dq, part_other, kv, low = call(
        functools.partial(first_kernel, chunks=late_chunks, group=group),
        (sel, docs, raw, tail, rows, grads),
        [SMEM] + [VMEM] * 5,
        [VMEM] * 4,
        [
            by_head(late_chunks),
            shape((2, shared, tokens, size), F32),
            shape((2, kv_count, rest, size), BF16),
            shape((2, chunks, CHUNK * group), jnp.int32),
        ],
        [],
        20,
        cost(half * len(late_chunks)),
    )

    def early(n, halo, extra, heads, staged_dq, emit):
        return call(
            functools.partial(early_kernel, group=group, n=n),
            (sel, docs, low, rows, grads, kv, halo, extra),
            [SMEM] + [VMEM] * 7,
            [VMEM] * 3,
            [staged_dq, shape((2, heads, WINDOW, size), emit), shape((2, heads, WINDOW, size), BF16)],
            [],
            20,
            cost(half * 2),
        )

    early_dq, first_other, back_other = early(0, halo_other, part_other, shared, by_head(early_chunks), BF16)
    back_other = shift(back_other, "ctx", -1)
    first_other = swap(first_other)
    own_late_dq, part_mine = call(
        functools.partial(late_kernel, chunks=late_chunks, group=group),
        (sel, low, rows, grads, lead, kv, tail),
        [SMEM] + [VMEM] * 6,
        [VMEM] * 2,
        [staged(late_chunks), shape((2, half, tokens, size), F32)],
        [],
        20,
        cost(half * len(late_chunks)),
    )
    own_early_dq, early_mine, back_mine = early(1, halo_mine, lead, half, staged(early_chunks), F32)
    back_mine = shift(back_mine, "ctx", -1)
    last_other = part_other[:, :, WINDOW:]
    last_other = last_other.at[:, :, tokens - 2 * WINDOW :].add(back_other.astype(F32)).astype(BF16)
    last_other = swap(last_other)
    query_grad = call(
        functools.partial(moved_kernel, chunks=late_chunks, group=group),
        (sel, docs, low, rows, grads, kv, tail, halo_mine, own_early_dq, own_late_dq, early_dq, late_dq),
        [SMEM] + [VMEM] * 11,
        ANY,
        shape(rows.shape, BF16),
        [pltpu.VMEM((chunks, CHUNK, half * group, size), BF16), dma((2 * chunks,))],
        20,
        cost(chunks),
    )
    out = shape((tokens, half, size), BF16)
    key_grad, value_grad = call(
        begin_kernel,
        (early_mine, first_other, part_mine),
        [VMEM] * 3,
        [ANY, ANY],
        [out, out],
        [pltpu.VMEM((2, WINDOW, half, size), BF16), dma((2,))],
        8,
    )
    key_grad, value_grad = call(
        finish_kernel,
        (part_mine, last_other, back_mine, key_grad, value_grad),
        [VMEM] * 3 + [ANY] * 2,
        [ANY, ANY],
        [out, out],
        [pltpu.VMEM((2, rest, half, size), BF16), dma((2, rest // CHUNK))],
        8,
        aliases={3: 0, 4: 1},
    )
    return query_grad.reshape(queries.shape), key_grad, value_grad


def solution(mesh):
    in_specs = (
        P("ctx", None, "head", None),
        P("ctx", None, None),
        P("ctx", None, None),
        P("ctx", None, "head", None),
        P("ctx"),
    )
    out_specs = (P("ctx", None, "head", None), P("ctx", "head", None), P("ctx", "head", None))

    return jax.shard_map(on_device, mesh=mesh, in_specs=in_specs, out_specs=out_specs, check_vma=False)
```
